128 devices in a mesh: row: 4 (over y), col: 4 (over x_hi, core), chol: 8 (over z, x_lo).
Axes of the slice: x: 4 (x_hi: 2, x_lo: 2; x = x_hi * 2 + x_lo), y: 4, z: 4, core: 2. Of those that a mesh axis runs over, the one named last changes fastest.
Arguments:
- left_vectors: bfloat16 [64, 4608, 1536], P(None, ('col', 'chol'), 'row'), may hold values from -0.75 to 0.75
- right_vectors: bfloat16 [16, 4608, 1536], P(None, ('col', 'chol'), 'row'), may hold values from -0.0234375 to 0.0234375
- amplitudes: bfloat16 [8, 16, 64], replicated, may hold values from -6 to 6
Outputs:
- ladder: float32 [8, 1536, 1536], P('chol', 'row', 'col')
The draws below stay inside these ranges and needn't reach their ends.
All inputs are finite; a program needn't handle non-finite values.
Results may differ from the reference program's by a relative error of at most 0.0029.
Values may be sent and summed in bfloat16 or wider, within the bound.
A program may use at most 128 MiB of HBM per device.

```python
import jax
import jax.numpy as jnp
from jax import lax

V = 1536
NVEC = 4608
CB = 64
DB = 16
IJ = 8


def level_of(own_key, shape, pieces, smallest, high):
    def one(dim, blocks):
        steps = jax.random.uniform(jax.random.fold_in(jax.random.fold_in(own_key, 6), dim), (blocks,), jnp.float32, smallest / len(pieces), high / len(pieces))
        return jnp.repeat(jnp.exp(steps), shape[dim] // blocks).reshape((-1,) + (1,) * (len(shape) - dim - 1))

    gain = one(*pieces[0])
    for cut in pieces[1:]:
        gain = gain * one(*cut)
    return gain


def centred(stream_key, dims, width, most, pieces=(), dtype=jnp.bfloat16):
    level = level_of(stream_key, dims, pieces, -0.22, 0.18) if pieces else 1.0
    entries = jax.random.normal(stream_key, dims, jnp.float32) * width * level
    return jnp.minimum(jnp.maximum(entries, -most), most).astype(dtype)


def setup_inputs(seed: int = 0) -> dict:
    streams_of = jax.random.split(jax.random.key(seed), 4)
    return {
        "left_vectors": centred(streams_of[0], (CB, NVEC, V), CB ** -0.5, 0.75, ((1, 32), (2, 4))),
        "right_vectors": centred(streams_of[1], (DB, NVEC, V), (NVEC * DB) ** -0.5, 0.0234375, ((1, 32), (2, 4))),
        "amplitudes": centred(streams_of[2], (IJ, DB, CB), 1.0, 6.0),
    }


def reference(left_vectors, right_vectors, amplitudes):
    c_block = left_vectors.shape[0]
    width_a = left_vectors.shape[2]
    left_flat = left_vectors.reshape(c_block, -1)
    right_flat = right_vectors.reshape(-1, right_vectors.shape[2])

    def one_pair(amp_rows):
        halved = jnp.dot(amp_rows, left_flat, preferred_element_type=jnp.float32).astype(jnp.bfloat16)
        halved = halved.reshape(-1, width_a)
        return lax.dot_general(halved, right_flat, (((0,), (0,)), ((), ())), preferred_element_type=jnp.float32)

    return lax.map(one_pair, amplitudes)
```

```python
import functools

import jax
import jax.numpy as jnp
from jax import lax
from jax.experimental import pallas as pl
from jax.experimental.pallas import tpu as pltpu
from jax.sharding import Mesh
from jax.sharding import PartitionSpec as P

COL = ("col_0", "col_1")
COL_CHOL = ("col_0", "col_1", "chol_0", "chol_1")
CHOL = ("chol_0", "chol_1")
MESH = pl.DeviceIdType.MESH
F32 = jnp.float32
BF16 = jnp.bfloat16
CH = 128
PB = 16

GROUPS = (
    ((0, 0), (0, 1)),
    ((0, 2),),
    ((3, 0), (1, 2)),
    ((3, 1), (1, 1)),
    ((3, 2), (1, 0)),
    ((2, 0), (2, 2)),
    ((2, 1),),
)
NG = len(GROUPS)
GATHERED = 2


def where():
    return dict(
        y=lax.axis_index("row"),
        x=lax.axis_index("col_0") * 2 + lax.axis_index("chol_1"),
        z=lax.axis_index("chol_0"),
        c=lax.axis_index("col_1"),
    )


def device(y, x, z, c):
    return (y, x // 2, c, z, lax.rem(x, 2))


def kernel(
    sizes, amp_ref, left_hbm, right_hbm, out_ref,
    left_buf, left_f32, right_buf, right_f32, own, got, halved, prod, core_got, chip, z_got,
    summed, x_got,
    load_sem, right_sem, ag_send, ag_recv, core_send, core_recv, z_send, z_recv, x_send, x_recv,
):
    pairs, d_block, c_block, vectors, width = sizes
    depth = d_block * vectors
    me = where()
    y, x, z, c = me["y"], me["x"], me["z"], me["c"]
    up = device(lax.rem(y + 1, 4), x, z, c)
    down = device(lax.rem(y + 3, 4), x, z, c)
    partner = device(y, x, z, 1 - c)

    barrier = pltpu.get_barrier_semaphore()
    others = [up, down, partner]
    others += [device(y, x, lax.rem(z + k, 4), c) for k in (1, 2, 3)]
    others += [device(y, lax.rem(x + k, 4), z, q) for k in (1, 2, 3) for q in (c, 1 - c)]
    for other in others:
        pl.semaphore_signal(barrier, inc=1, device_id=other, device_id_type=MESH)

    load_right = pltpu.make_async_copy(right_hbm, right_buf, right_sem)
    load_right.start()

    def load_left(block, slot):
        return pltpu.make_async_copy(
            left_hbm.at[:, pl.ds(pl.multiple_of(block * PB, PB), PB), :],
            left_buf.at[slot],
            load_sem.at[slot],
        )

    load_left(0, 0).start()
    load_right.wait()

    def turn(chunk):
        lanes = slice(chunk * CH, (chunk + 1) * CH)

        @pl.loop(0, d_block)
        def _(d):
            right_f32[pl.ds(d * vectors, vectors), :] = right_buf[d, :, lanes].astype(F32)

        @pl.loop(0, depth // CH)
        def _(k):
            vecs = CH // d_block
            rows = [
                right_f32[pl.ds(k * vecs + p, d_block, stride=vectors), :] for p in range(vecs)
            ]
            block = jnp.concatenate(rows, axis=0)
            at = pl.multiple_of(k * CH, CH)
            own[pl.ds(chunk * CH, CH), pl.ds(at, CH)] = block.T.astype(BF16)

    def remote(src, dst, send, recv, target):
        return pltpu.make_async_remote_copy(
            src_ref=src, dst_ref=dst, send_sem=send, recv_sem=recv, device_id=target,
            device_id_type=MESH,
        )

    def gather_copy(way, k):
        target = up if way == 0 else down
        at = way * CH
        if k < 3:
            chunk = k if way == 0 else 2 - k
            src = own.at[pl.ds(chunk * CH, CH), :]
            dst = got.at[k, pl.ds(at, CH), :]
        elif k == 3:
            src = got.at[0, pl.ds(at, CH), :]
            dst = got.at[3, pl.ds(at, CH), :]
        else:
            half = CH // 2
            src = got.at[1, pl.ds(at + way * half, half), :]
            dst = got.at[4, pl.ds(way * half, half), :]
        return remote(src, dst, ag_send.at[way, k], ag_recv.at[way, k], target)

    turn(0)
    pl.semaphore_wait(barrier, len(others))
    gather_copy(0, 0).start()
    turn(2)
    gather_copy(1, 0).start()
    turn(1)
    gather_copy(0, 1).start()
    gather_copy(1, 1).start()
    gather_copy(0, 2).start()
    gather_copy(1, 2).start()

    @pl.loop(0, vectors // PB)
    def _(block):
        slot = lax.rem(block, 2)
        load_left(block, slot).wait()

        @pl.when(block + 1 < vectors // PB)
        def _():
            load_left(block + 1, 1 - slot).start()

        @pl.loop(0, c_block // 8)
        def _(k):
            part = left_buf[slot, pl.ds(k * 8, 8)].astype(F32)
            for lane in range(width // 128):
                left_f32[lane, pl.ds(pl.multiple_of(k * 8 * PB, 8 * PB), 8 * PB), :] = part[
                    :, :, lane * 128 : (lane + 1) * 128
                ].reshape(8 * PB, 128)

        @pl.loop(0, PB // 2)
        def _(k):
            cols = [
                left_f32[lane, pl.ds(2 * k + q, c_block, stride=PB), :]
                for q in range(2)
                for lane in range(width // 128)
            ]
            vecs = jnp.concatenate(cols, axis=1).astype(BF16)
            half = jnp.dot(amp_ref[...], vecs, preferred_element_type=F32).astype(BF16)
            for q in range(2):
                at = pl.multiple_of((block * PB + 2 * k + q) * d_block, d_block)
                for ij in range(pairs):
                    halved[ij // 2, pl.ds(at, d_block), (ij % 2) * width : (ij % 2 + 1) * width] = (
                        half[ij * d_block : (ij + 1) * d_block, q * width : (q + 1) * width]
                    )

    rows_of = [CH * len(parts) for parts in GROUPS]
    start_of = [sum(rows_of[:g]) for g in range(NG)]

    def core_copy(g):
        lanes = pl.ds(pl.multiple_of((1 - c) * width, 128), width)
        return remote(
            prod.at[g % 2, :, pl.ds(0, rows_of[g]), lanes],
            core_got.at[:, pl.ds(start_of[g], rows_of[g]), :],
            core_send.at[g],
            core_recv.at[g],
            partner,
        )

    def multiply(g):
        rows = rows_of[g]
        if g < GATHERED:
            panel = own.at[pl.ds(start_of[g], rows), :]
        else:
            panel = got.at[g - GATHERED, pl.ds(0, rows), :]

        @pl.loop(0, (pairs // 2) * (2 * width // 256))
        def _(n):
            zz = n // (2 * width // 256)
            at = pl.multiple_of(lax.rem(n, 2 * width // 256) * 256, 256)
            prod[g % 2, zz, pl.ds(0, rows), pl.ds(at, 256)] = jnp.dot(
                panel[...], halved[zz, :, pl.ds(at, 256)], preferred_element_type=F32
            )

        core_copy(g).start()

    def z_copy(g, k):
        zz = lax.rem(z + k, 4)
        span = pl.ds(start_of[g], rows_of[g])
        return remote(
            chip.at[zz, span, :],
            z_got.at[k - 1, span, :],
            z_send.at[g, k - 1],
            z_recv.at[g, k - 1],
            device(y, x, zz, c),
        )

    def chip_sum(g):
        core_copy(g).wait()
        lanes = pl.ds(pl.multiple_of(c * width, 128), width)

        @pl.loop(0, (pairs // 2) * (rows_of[g] // 32))
        def _(n):
            zz = n // (rows_of[g] // 32)
            r = pl.multiple_of(lax.rem(n, rows_of[g] // 32) * 32, 32)
            total = prod[g % 2, zz, pl.ds(r, 32), lanes] + core_got[
                zz, pl.ds(start_of[g] + r, 32), :
            ]
            chip[zz, pl.ds(start_of[g] + r, 32), :] = total.astype(BF16)

        for k in (2, 1, 3):
            z_copy(g, k).start()

    def x_copy(g, i):
        offset, chunk = GROUPS[g][i]
        tile = lax.rem(y + offset, 4)
        span = pl.ds(start_of[g] + i * CH, CH)
        src = summed.at[span, :]
        dst = x_got.at[x, pl.ds(chunk * CH, CH), :]
        to_x, to_c = 2 * (tile // 2) + c, lax.rem(tile, 2)
        mine = jnp.logical_and(to_x == x, to_c == c)
        send, recv = x_send.at[g, i], x_recv.at[chunk, x]
        away = remote(src, dst, send, recv, device(y, to_x, z, to_c))
        here = pltpu.make_async_copy(src, dst, recv)
        return mine, away, here

    def z_sum(g):
        for k in (1, 2, 3):
            z_copy(g, k).wait_recv()

        @pl.loop(0, rows_of[g] // 32)
        def _(n):
            span = pl.ds(pl.multiple_of(start_of[g] + n * 32, 32), 32)
            total = chip[z, span, :].astype(F32)
            for k in range(3):
                total = total + z_got[k, span, :].astype(F32)
            summed[span, :] = total.astype(BF16)

        for i in range(len(GROUPS[g])):
            mine, away, here = x_copy(g, i)

            @pl.when(mine)
            def _():
                here.start()

            @pl.when(jnp.logical_not(mine))
            def _():
                away.start()

    own_tile = 2 * (x // 2) + c
    own_offset = lax.rem(own_tile - y + 4, 4)

    def x_sum(g):
        for offset, chunk in GROUPS[g]:

            @pl.when(own_offset == offset)
            def _():
                for k in range(4):
                    dst = x_got.at[k, pl.ds(chunk * CH, CH), :]
                    pltpu.make_async_copy(dst, dst, x_recv.at[chunk, k]).wait()

                @pl.loop(0, CH // 32)
                def _(n):
                    span = pl.ds(pl.multiple_of(chunk * CH + n * 32, 32), 32)
                    total = x_got[0, span, :].astype(F32)
                    for k in range(1, 4):
                        total = total + x_got[k, span, :].astype(F32)
                    out_ref[span, :] = total

    for g in range(NG):
        if g >= GATHERED:
            k = g - GATHERED
            for way in range(2):
                gather_copy(way, k).wait_recv()
            if k < 2:
                for way in range(2):
                    gather_copy(way, k + 3).start()
        multiply(g)
        chip_sum(g)
        if g >= 1:
            z_sum(g - 1)
        if g >= 2:
            x_sum(g - 2)
    z_sum(NG - 1)
    x_sum(NG - 2)
    x_sum(NG - 1)

    for way in range(2):
        for k in range(5):
            gather_copy(way, k).wait_send()
    for g in range(NG):
        for k in (1, 2, 3):
            z_copy(g, k).wait_send()
        for i in range(len(GROUPS[g])):
            mine, away, _ = x_copy(g, i)

            @pl.when(jnp.logical_not(mine))
            def _():
                away.wait_send()


def shards(left_vectors, right_vectors, amplitudes):
    pairs, d_block, c_block = amplitudes.shape
    _, vectors, width = left_vectors.shape
    depth = d_block * vectors
    rows = CH * sum(len(parts) for parts in GROUPS)
    big = 2 * CH
    dma = pltpu.SemaphoreType.DMA
    turned = pl.pallas_call(
        functools.partial(kernel, (pairs, d_block, c_block, vectors, width)),
        out_shape=jax.ShapeDtypeStruct((width, width), F32),
        in_specs=[
            pl.BlockSpec(memory_space=pltpu.VMEM),
            pl.BlockSpec(memory_space=pl.ANY),
            pl.BlockSpec(memory_space=pl.ANY),
        ],
        out_specs=pl.BlockSpec(memory_space=pltpu.VMEM),
        scratch_shapes=[
            pltpu.VMEM((2, c_block, PB, width), BF16),
            pltpu.VMEM((width // 128, c_block * PB, 128), F32),
            pltpu.VMEM((d_block, vectors, width), BF16),
            pltpu.VMEM((depth, CH), F32),
            pltpu.VMEM((width, depth), BF16),
            pltpu.VMEM((5, big, depth), BF16),
            pltpu.VMEM((pairs // 2, depth, 2 * width), BF16),
            pltpu.VMEM((2, pairs // 2, big, 2 * width), F32),
            pltpu.VMEM((pairs // 2, rows, width), F32),
            pltpu.VMEM((pairs // 2, rows, width), BF16),
            pltpu.VMEM((3, rows, width), BF16),
            pltpu.VMEM((rows, width), BF16),
            pltpu.VMEM((4, width, width), BF16),
            dma((2,)),
            dma,
            dma((2, 5)),
            dma((2, 5)),
            dma((NG,)),
            dma((NG,)),
            dma((NG, 3)),
            dma((NG, 3)),
            dma((NG, 2)),
            dma((3, 4)),
        ],
        compiler_params=pltpu.CompilerParams(
            collective_id=0, has_side_effects=True, vmem_limit_bytes=67_043_328
        ),
    )(amplitudes.reshape(pairs * d_block, c_block), left_vectors, right_vectors)
    return turned.T[None]


def solution(mesh):
    finer = Mesh(
        mesh.devices.reshape(mesh.shape["row"], 2, 2, 4, 2),
        ("row", "col_0", "col_1", "chol_0", "chol_1"),
    )
    placed = (P(None, COL_CHOL, "row"), P(None, COL_CHOL, "row"), P())
    return jax.shard_map(
        shards, mesh=finer, in_specs=placed, out_specs=P(CHOL, "row", COL), check_vma=False
    )
```

```python
import functools

import jax
import jax.numpy as jnp
from jax import lax
from jax.experimental import pallas as pl
from jax.experimental.pallas import tpu as pltpu
from jax.sharding import Mesh
from jax.sharding import PartitionSpec as P

COL = ("col_0", "col_1")
COL_CHOL = ("col_0", "col_1", "chol_0", "chol_1")
CHOL = ("chol_0", "chol_1")
MESH = pl.DeviceIdType.MESH
F32 = jnp.float32
BF16 = jnp.bfloat16
CH = 128
PB = 16

GROUPS = (
    ((0, 0, 256, "z"),),
    ((0, 256, 128, "z"),),
    ((3, 0, 128, "x"), (1, 256, 128, "x")),
    ((3, 128, 128, "z"), (1, 128, 128, "z")),
    ((2, 0, 128, "z"), (2, 256, 128, "x")),
    ((2, 128, 128, "z"),),
    ((3, 256, 64, "x"), (1, 0, 64, "x")),
    ((3, 320, 32, "z"), (3, 352, 32, "x"), (1, 64, 32, "z"), (1, 96, 32, "x")),
)
NG = len(GROUPS)
GATHERED = 2


class Part:
    def __init__(self, number, group, offset, tile_row, rows, first, row, row_z, row_x):
        self.number, self.group, self.offset, self.tile_row = number, group, offset, tile_row
        self.rows, self.first, self.row, self.row_z, self.row_x = rows, first, row, row_z, row_x


def laid_out():
    parts, row, row_z, row_x = [], 0, 0, 0
    for g, group in enumerate(GROUPS):
        shared = 0
        for offset, tile_row, rows, first in group:
            parts.append(Part(len(parts), g, offset, tile_row, rows, first, row, row_z, row_x))
            row += rows
            if first == "z":
                row_z += rows
            else:
                shared = rows
        row_x += shared
    return parts, row, row_z, row_x


PARTS, ROWS, ROWS_Z, ROWS_X = laid_out()


def where():
    return dict(
        y=lax.axis_index("row"),
        x=lax.axis_index("col_0") * 2 + lax.axis_index("chol_1"),
        z=lax.axis_index("chol_0"),
        c=lax.axis_index("col_1"),
    )


def device(y, x, z, c):
    return (y, x // 2, c, z, lax.rem(x, 2))


def kernel(
    sizes, amp_ref, left_hbm, right_hbm, out_ref,
    left_buf, left_f32, right_buf, right_f32, own, got, halved, prod, core_got, chip, z_got,
    z_total, x_got, x_total, last_got,
    load_sem, right_sem, ag_send, ag_recv, core_send, core_recv, z_send, z_recv, x_send, x_recv,
    last_send, last_recv,
):
    pairs, d_block, c_block, vectors, width = sizes
    depth = d_block * vectors
    me = where()
    y, x, z, c = me["y"], me["x"], me["z"], me["c"]
    up = device(lax.rem(y + 1, 4), x, z, c)
    down = device(lax.rem(y + 3, 4), x, z, c)
    partner = device(y, x, z, 1 - c)

    barrier = pltpu.get_barrier_semaphore()
    others = [up, down, partner]
    others += [device(y, x, lax.rem(z + k, 4), q) for k in (1, 2, 3) for q in (c, 1 - c)]
    others += [device(y, lax.rem(x + k, 4), z, q) for k in (1, 2, 3) for q in (c, 1 - c)]
    for other in others:
        pl.semaphore_signal(barrier, inc=1, device_id=other, device_id_type=MESH)

    def load_right(chunk):
        lanes = pl.ds(chunk * CH, CH)
        return pltpu.make_async_copy(
            right_hbm.at[:, :, lanes], right_buf.at[chunk], right_sem.at[chunk]
        )

    for chunk in (0, 2, 1):
        load_right(chunk).start()

    def load_left(block, slot):
        return pltpu.make_async_copy(
            left_hbm.at[:, pl.ds(pl.multiple_of(block * PB, PB), PB), :],
            left_buf.at[slot],
            load_sem.at[slot],
        )

    load_left(0, 0).start()

    def turn(chunk):
        load_right(chunk).wait()

        @pl.loop(0, d_block, unroll=4)
        def _(d):
            right_f32[pl.ds(d * vectors, vectors), :] = right_buf[chunk, d].astype(F32)

        @pl.loop(0, depth // CH, unroll=6)
        def _(k):
            vecs = CH // d_block
            rows = [
                right_f32[pl.ds(k * vecs + p, d_block, stride=vectors), :] for p in range(vecs)
            ]
            block = jnp.concatenate(rows, axis=0).astype(BF16)
            own[pl.ds(chunk * CH, CH), pl.ds(pl.multiple_of(k * CH, CH), CH)] = block.T

    def remote(src, dst, send, recv, target):
        return pltpu.make_async_remote_copy(
            src_ref=src, dst_ref=dst, send_sem=send, recv_sem=recv, device_id=target,
            device_id_type=MESH,
        )

    rows_of = [sum(p.rows for p in PARTS if p.group == g) for g in range(NG)]
    start_of = [sum(rows_of[:g]) for g in range(NG)]

    def gather_copy(way, k):
        target = up if way == 0 else down
        first = start_of[GATHERED]
        half = rows_of[GATHERED + k] // 2
        dst = got.at[pl.ds(start_of[GATHERED + k] - first + way * half, half), :]
        if k in (2, 3):
            at = start_of[GATHERED + k - 2] - first + way * CH + (way * half if k == 3 else 0)
            src = got.at[pl.ds(at, half), :]
        else:
            chunk = min(k, 2) if way == 0 else 2 - min(k, 2)
            src = own.at[pl.ds(chunk * CH + (half if k == 5 else 0), half), :]
        return remote(src, dst, ag_send.at[way, k], ag_recv.at[way, k], target)

    turn(0)
    pl.semaphore_wait(barrier, len(others))
    gather_copy(0, 0).start()
    turn(2)
    gather_copy(1, 0).start()
    turn(1)
    gather_copy(0, 1).start()
    gather_copy(1, 1).start()

    @pl.loop(0, vectors // PB)
    def _(block):
        slot = lax.rem(block, 2)
        load_left(block, slot).wait()

        @pl.when(block + 1 < vectors // PB)
        def _():
            load_left(block + 1, 1 - slot).start()

        @pl.loop(0, c_block // 8, unroll=4)
        def _(k):
            part = left_buf[slot, pl.ds(k * 8, 8)].astype(F32)
            for lane in range(width // 128):
                left_f32[lane, pl.ds(pl.multiple_of(k * 8 * PB, 8 * PB), 8 * PB), :] = part[
                    :, :, lane * 128 : (lane + 1) * 128
                ].reshape(8 * PB, 128)

        @pl.loop(0, PB // 2, unroll=8)
        def _(k):
            cols = [
                left_f32[lane, pl.ds(2 * k + q, c_block, stride=PB), :]
                for q in range(2)
                for lane in range(width // 128)
            ]
            vecs = jnp.concatenate(cols, axis=1).astype(BF16)
            half = jnp.dot(amp_ref[...], vecs, preferred_element_type=F32).astype(BF16)
            for q in range(2):
                at = pl.multiple_of((block * PB + 2 * k + q) * d_block, d_block)
                for ij in range(pairs):
                    halved[ij // 2, pl.ds(at, d_block), (ij % 2) * width : (ij % 2 + 1) * width] = (
                        half[ij * d_block : (ij + 1) * d_block, q * width : (q + 1) * width]
                    )

    halves = pairs // 2
    step = 64

    def core_copy(g, zz):
        lanes = pl.ds(pl.multiple_of((1 - c) * width, 128), width)
        return remote(
            prod.at[g % 2, zz, pl.ds(0, rows_of[g]), lanes],
            core_got.at[zz, pl.ds(start_of[g], rows_of[g]), :],
            core_send.at[g, zz],
            core_recv.at[g, zz],
            partner,
        )

    def multiply(g):
        rows = rows_of[g]
        if g < GATHERED:
            panel = own.at[pl.ds(start_of[g], rows), :]
        else:
            panel = got.at[pl.ds(start_of[g] - start_of[GATHERED], rows), :]

        @pl.loop(0, halves, unroll=2 if rows > CH else 4)
        def _(i):
            zz = lax.rem(z + 1 + i, 4)
            prod[g % 2, zz, pl.ds(0, rows), :] = jnp.dot(
                panel[...], halved[zz], preferred_element_type=F32
            )
            core_copy(g, zz).start()

    def place(part):
        tile = lax.rem(y + part.offset, 4)
        return tile // 2, lax.rem(tile, 2)

    def z_copy(part, k):
        zz = lax.rem(z + k, 4)
        return remote(
            chip.at[zz, pl.ds(part.row, part.rows), :],
            z_got.at[k - 1, pl.ds(part.row_z, part.rows), :],
            z_send.at[part.number, k - 1],
            z_recv.at[part.number, k - 1],
            device(y, x, zz, c),
        )

    def x_copy(part, zz):
        to_x = 2 * place(part)[0] + c
        slot = lax.rem(x - to_x + 7, 4)
        return to_x != x, remote(
            chip.at[zz, pl.ds(part.row, part.rows), :],
            x_got.at[slot, zz, pl.ds(part.row_x, part.rows), :],
            x_send.at[part.number, zz],
            x_recv.at[part.group, slot, zz],
            device(y, to_x, z, c),
        )

    def sums_over_x(part):
        return 2 * place(part)[0] + c == x

    def chip_sum(g):
        lanes = pl.ds(pl.multiple_of(c * width, 128), width)
        for i in range(halves):
            zz = lax.rem(z + 1 + i, 4)
            core_copy(g, zz).wait()

            @pl.loop(0, rows_of[g] // step)
            def _(n):
                r = pl.multiple_of(n * step, step)
                at = pl.ds(pl.multiple_of(start_of[g] + r, step), step)
                total = prod[g % 2, zz, pl.ds(r, step), lanes] + core_got[zz, at, :]
                chip[zz, at, :] = total.astype(BF16)

            for part in PARTS:
                if part.group != g:
                    continue
                if part.first == "z":
                    if i < halves - 1:
                        z_copy(part, i + 1).start()
                else:
                    away, copy = x_copy(part, zz)

                    @pl.when(away)
                    def _():
                        copy.start()

    def last_copies(part):
        to_c = place(part)[1]
        if part.first == "z":
            to_x = 2 * place(part)[0] + c
            ends = [(z_total.at[pl.ds(part.row_z, part.rows), :], x, to_x, z)]
        else:
            ends = [
                (x_total.at[zz, pl.ds(part.row_x, part.rows), :], z, x, zz) for zz in range(halves)
            ]
        copies = []
        for k, (src, slot, to_x, to_z) in enumerate(ends):
            dst = last_got.at[slot, pl.ds(part.tile_row, part.rows), :]
            recv = last_recv.at[part.number, slot]
            mine = jnp.logical_and(jnp.logical_and(to_x == x, to_z == z), to_c == c)
            away = remote(
                src, dst, last_send.at[part.number, k], recv, device(y, to_x, to_z, to_c)
            )
            copies.append((mine, away, pltpu.make_async_copy(src, dst, recv)))
        return copies

    def send_last(part):
        for mine, away, here in last_copies(part):

            @pl.when(mine)
            def _():
                here.start()

            @pl.when(jnp.logical_not(mine))
            def _():
                away.start()

    def wait_last(part):
        for mine, away, _ in last_copies(part):

            @pl.when(jnp.logical_not(mine))
            def _():
                away.wait_send()

    def second(g):
        for part in PARTS:
            if part.group != g:
                continue
            if part.first == "z":
                for k in (1, 2, 3):
                    z_copy(part, k).wait_recv()

                step = min(part.rows, 64)

                @pl.loop(0, part.rows // step)
                def _(n):
                    total = chip[z, pl.ds(part.row + n * step, step), :].astype(F32)
                    at = pl.ds(part.row_z + n * step, step)
                    for k in range(3):
                        total = total + z_got[k, at, :].astype(F32)
                    z_total[at, :] = total.astype(BF16)

                send_last(part)
            else:

                @pl.when(sums_over_x(part))
                def _():
                    at = pl.ds(part.row_x, part.rows)
                    step = min(part.rows, 64)
                    for k in range(3):
                        for zz in range(halves):
                            dst = x_got.at[k, zz, at, :]
                            pltpu.make_async_copy(dst, dst, x_recv.at[g, k, zz]).wait()

                    @pl.loop(0, halves * (part.rows // step))
                    def _(n):
                        zz, r = n // (part.rows // step), lax.rem(n, part.rows // step) * step
                        r = pl.multiple_of(r, step)
                        total = chip[zz, pl.ds(part.row + r, step), :].astype(F32)
                        at = pl.ds(part.row_x + r, step)
                        for k in range(3):
                            total = total + x_got[k, zz, at, :].astype(F32)
                        x_total[zz, at, :] = total.astype(BF16)

                    send_last(part)

    own_tile = 2 * (x // 2) + c
    own_offset = lax.rem(own_tile - y + 4, 4)

    def final(g):
        for part in PARTS:
            if part.group != g:
                continue

            @pl.when(own_offset == part.offset)
            def _():
                for k in range(4):
                    dst = last_got.at[k, pl.ds(part.tile_row, part.rows), :]
                    pltpu.make_async_copy(dst, dst, last_recv.at[part.number, k]).wait()

                step = min(part.rows, 64)

                @pl.loop(0, part.rows // step)
                def _(n):
                    at = pl.ds(part.tile_row + n * step, step)
                    total = last_got[0, at, :].astype(F32)
                    for k in range(1, 4):
                        total = total + last_got[k, at, :].astype(F32)
                    out_ref[at, :] = total

    for g in range(NG):
        if g >= GATHERED:
            k = g - GATHERED
            for way in range(2):
                gather_copy(way, k).wait_recv()
            if k < 2:
                for step_on in ((2,), (3, 4, 5))[k]:
                    for way in range(2):
                        gather_copy(way, step_on).start()
        multiply(g)
        chip_sum(g)
        if g >= 1:
            second(g - 1)
        if g >= 2:
            final(g - 2)
    second(NG - 1)
    final(NG - 2)
    final(NG - 1)

    for way in range(2):
        for k in range(6):
            gather_copy(way, k).wait_send()
    for part in PARTS:
        if part.first == "z":
            for k in (1, 2, 3):
                z_copy(part, k).wait_send()
            wait_last(part)
        else:
            for zz in range(halves):
                away, copy = x_copy(part, zz)

                @pl.when(away)
                def _():
                    copy.wait_send()

            @pl.when(sums_over_x(part))
            def _():
                wait_last(part)


def shards(left_vectors, right_vectors, amplitudes):
    pairs, d_block, c_block = amplitudes.shape
    _, vectors, width = left_vectors.shape
    depth = d_block * vectors
    big = 2 * CH
    dma = pltpu.SemaphoreType.DMA
    turned = pl.pallas_call(
        functools.partial(kernel, (pairs, d_block, c_block, vectors, width)),
        out_shape=jax.ShapeDtypeStruct((width, width), F32),
        in_specs=[
            pl.BlockSpec(memory_space=pltpu.VMEM),
            pl.BlockSpec(memory_space=pl.ANY),
            pl.BlockSpec(memory_space=pl.ANY),
        ],
        out_specs=pl.BlockSpec(memory_space=pltpu.VMEM),
        scratch_shapes=[
            pltpu.VMEM((2, c_block, PB, width), BF16),
            pltpu.VMEM((width // 128, c_block * PB, 128), F32),
            pltpu.VMEM((width // CH, d_block, vectors, CH), BF16),
            pltpu.VMEM((depth, CH), F32),
            pltpu.VMEM((width, depth), BF16),
            pltpu.VMEM((ROWS - width, depth), BF16),
            pltpu.VMEM((pairs // 2, depth, 2 * width), BF16),
            pltpu.VMEM((2, pairs // 2, big, 2 * width), F32),
            pltpu.VMEM((pairs // 2, ROWS, width), F32),
            pltpu.VMEM((pairs // 2, ROWS, width), BF16),
            pltpu.VMEM((3, ROWS_Z, width), BF16),
            pltpu.VMEM((ROWS_Z, width), BF16),
            pltpu.VMEM((3, pairs // 2, ROWS_X, width), BF16),
            pltpu.VMEM((pairs // 2, ROWS_X, width), BF16),
            pltpu.VMEM((4, width, width), BF16),
            dma((2,)),
            dma((width // CH,)),
            dma((2, 6)),
            dma((2, 6)),
            dma((NG, pairs // 2)),
            dma((NG, pairs // 2)),
            dma((len(PARTS), 3)),
            dma((len(PARTS), 3)),
            dma((len(PARTS), pairs // 2)),
            dma((NG, 3, pairs // 2)),
            dma((len(PARTS), 4)),
            dma((len(PARTS), 4)),
        ],
        compiler_params=pltpu.CompilerParams(
            collective_id=0, has_side_effects=True, vmem_limit_bytes=67_043_328
        ),
    )(amplitudes.reshape(pairs * d_block, c_block), left_vectors, right_vectors)
    return turned.T[None]


def solution(mesh):
    finer = Mesh(
        mesh.devices.reshape(mesh.shape["row"], 2, 2, 4, 2),
        ("row", "col_0", "col_1", "chol_0", "chol_1"),
    )
    placed = (P(None, COL_CHOL, "row"), P(None, COL_CHOL, "row"), P())
    return jax.shard_map(
        shards, mesh=finer, in_specs=placed, out_specs=P(CHOL, "row", COL), check_vma=False
    )
```

```python
import functools

import jax
import jax.numpy as jnp
from jax import lax
from jax.experimental import pallas as pl
from jax.experimental.pallas import tpu as pltpu
from jax.sharding import Mesh
from jax.sharding import PartitionSpec as P

COL = ("col_0", "col_1")
COL_CHOL = ("col_0", "col_1", "chol_0", "chol_1")
CHOL = ("chol_0", "chol_1")
MESH = pl.DeviceIdType.MESH
F32 = jnp.float32
BF16 = jnp.bfloat16
CH = 128
PB = 16

GROUPS = (
    ((0, 0, 256, "z"),),
    ((0, 256, 128, "z"),),
    ((3, 0, 128, "x"), (1, 256, 128, "x")),
    ((3, 128, 128, "z"), (1, 128, 128, "z")),
    ((2, 0, 128, "z"), (2, 256, 128, "z")),
    ((2, 128, 128, "z"),),
    ((3, 256, 64, "x"), (1, 0, 64, "x")),
    ((3, 320, 64, "z"), (1, 64, 64, "z")),
)
NG = len(GROUPS)
GATHERED = 2
ORDER = (
    ("mul", 0), ("mul", 1), ("chip", 0), ("chip", 1),
    ("get", 2), ("mul", 2), ("chip", 2),
    ("get", 3), ("mul", 3), ("second", 0), ("chip", 3), ("second", 1), ("second", 2),
    ("final", 0), ("final", 1),
    ("get", 4), ("mul", 4), ("chip", 4), ("second", 3), ("final", 2),
    ("get", 5), ("mul", 5), ("chip", 5),
    ("get", 6), ("mul", 6), ("chip", 6), ("second", 4),
    ("get", 7), ("mul", 7), ("chip", 7), ("second", 5), ("final", 3), ("second", 6), ("final", 4),
    ("second", 7), ("final", 5), ("final", 6), ("final", 7),
)


class Part:
    def __init__(self, number, group, offset, tile_row, rows, first, row, row_z, row_x):
        self.number, self.group, self.offset, self.tile_row = number, group, offset, tile_row
        self.rows, self.first, self.row, self.row_z, self.row_x = rows, first, row, row_z, row_x


def laid_out():
    parts, row, row_z, row_x = [], 0, 0, 0
    for g, group in enumerate(GROUPS):
        shared = 0
        for offset, tile_row, rows, first in group:
            parts.append(Part(len(parts), g, offset, tile_row, rows, first, row, row_z, row_x))
            row += rows
            if first == "z":
                row_z += rows
            else:
                shared = rows
        row_x += shared
    return parts, row, row_z, row_x


PARTS, ROWS, ROWS_Z, ROWS_X = laid_out()


def where():
    return dict(
        y=lax.axis_index("row"),
        x=lax.axis_index("col_0") * 2 + lax.axis_index("chol_1"),
        z=lax.axis_index("chol_0"),
        c=lax.axis_index("col_1"),
    )


def device(y, x, z, c):
    return (y, x // 2, c, z, lax.rem(x, 2))


def kernel(
    sizes, amp_ref, left_hbm, right_hbm, out_ref,
    left_buf, left_f32, right_buf, right_f32, own, got, halved, prod, core_got, chip, z_got,
    z_total, x_got, x_total, last_got,
    load_sem, right_sem, ag_send, ag_recv, core_send, core_recv, z_send, z_recv, x_send, x_recv,
    last_send, last_recv,
):
    pairs, d_block, c_block, vectors, width = sizes
    depth = d_block * vectors
    me = where()
    y, x, z, c = me["y"], me["x"], me["z"], me["c"]
    up = device(lax.rem(y + 1, 4), x, z, c)
    down = device(lax.rem(y + 3, 4), x, z, c)
    partner = device(y, x, z, 1 - c)

    barrier = pltpu.get_barrier_semaphore()
    others = [up, down, partner]
    others += [device(y, x, lax.rem(z + k, 4), q) for k in (1, 2, 3) for q in (c, 1 - c)]
    others += [device(y, lax.rem(x + k, 4), z, q) for k in (1, 2, 3) for q in (c, 1 - c)]
    for other in others:
        pl.semaphore_signal(barrier, inc=1, device_id=other, device_id_type=MESH)

    def load_right(chunk):
        lanes = pl.ds(chunk * CH, CH)
        return pltpu.make_async_copy(
            right_hbm.at[:, :, lanes], right_buf.at[chunk], right_sem.at[chunk]
        )

    for chunk in (0, 2, 1):
        load_right(chunk).start()

    def load_left(block, slot):
        return pltpu.make_async_copy(
            left_hbm.at[:, pl.ds(pl.multiple_of(block * PB, PB), PB), :],
            left_buf.at[slot],
            load_sem.at[slot],
        )

    load_left(0, 0).start()

    def turn(chunk):
        load_right(chunk).wait()

        @pl.loop(0, d_block, unroll=4)
        def _(d):
            right_f32[pl.ds(d * vectors, vectors), :] = right_buf[chunk, d].astype(F32)

        @pl.loop(0, depth // CH, unroll=6)
        def _(k):
            vecs = CH // d_block
            rows = [
                right_f32[pl.ds(k * vecs + p, d_block, stride=vectors), :] for p in range(vecs)
            ]
            block = jnp.concatenate(rows, axis=0).astype(BF16)
            own[pl.ds(chunk * CH, CH), pl.ds(pl.multiple_of(k * CH, CH), CH)] = block.T

    def remote(src, dst, send, recv, target):
        return pltpu.make_async_remote_copy(
            src_ref=src, dst_ref=dst, send_sem=send, recv_sem=recv, device_id=target,
            device_id_type=MESH,
        )

    rows_of = [sum(p.rows for p in PARTS if p.group == g) for g in range(NG)]
    start_of = [sum(rows_of[:g]) for g in range(NG)]

    def landed(ref, sem):
        pltpu.make_async_copy(ref, ref, sem).wait()

    def gather_copy(way, k):
        target = up if way == 0 else down
        first = start_of[GATHERED]
        half = rows_of[GATHERED + k] // 2
        dst = got.at[pl.ds(start_of[GATHERED + k] - first + way * half, half), :]
        if k in (2, 3):
            at = start_of[GATHERED + k - 2] - first + way * CH + (way * half if k == 3 else 0)
            src = got.at[pl.ds(at, half), :]
        else:
            chunk = min(k, 2) if way == 0 else 2 - min(k, 2)
            past = sum(rows_of[GATHERED + 4 : GATHERED + k]) // 2
            src = own.at[pl.ds(chunk * CH + past, half), :]
        return remote(src, dst, ag_send.at[way], ag_recv.at[k], target)

    turn(0)
    pl.semaphore_wait(barrier, len(others))
    gather_copy(0, 0).start()
    turn(2)
    gather_copy(1, 0).start()
    turn(1)
    gather_copy(0, 1).start()
    gather_copy(1, 1).start()

    @pl.loop(0, vectors // PB)
    def _(block):
        slot = lax.rem(block, 2)
        load_left(block, slot).wait()

        @pl.when(block + 1 < vectors // PB)
        def _():
            load_left(block + 1, 1 - slot).start()

        @pl.loop(0, c_block // 8, unroll=4)
        def _(k):
            part = left_buf[slot, pl.ds(k * 8, 8)].astype(F32)
            for lane in range(width // 128):
                left_f32[lane, pl.ds(pl.multiple_of(k * 8 * PB, 8 * PB), 8 * PB), :] = part[
                    :, :, lane * 128 : (lane + 1) * 128
                ].reshape(8 * PB, 128)

        @pl.loop(0, PB // 2, unroll=8)
        def _(k):
            cols = [
                left_f32[lane, pl.ds(2 * k + q, c_block, stride=PB), :]
                for q in range(2)
                for lane in range(width // 128)
            ]
            vecs = jnp.concatenate(cols, axis=1).astype(BF16)
            half = jnp.dot(amp_ref[...], vecs, preferred_element_type=F32).astype(BF16)
            for q in range(2):
                at = pl.multiple_of((block * PB + 2 * k + q) * d_block, d_block)
                for ij in range(pairs):
                    halved[ij // 2, pl.ds(at, d_block), (ij % 2) * width : (ij % 2 + 1) * width] = (
                        half[ij * d_block : (ij + 1) * d_block, q * width : (q + 1) * width]
                    )

    halves = pairs // 2
    step = 64

    def core_copy(g, pair, zz):
        lanes = pl.ds(pl.multiple_of((1 - c) * width, 128), width)
        return remote(
            prod.at[g % 2, zz, pl.ds(0, rows_of[g]), lanes],
            core_got.at[zz, pl.ds(start_of[g], rows_of[g]), :],
            core_send.at[g % 2, pair],
            core_recv.at[g, pair],
            partner,
        )

    def multiply(g):
        rows = rows_of[g]
        if g < GATHERED:
            panel = own.at[pl.ds(start_of[g], rows), :]
        else:
            panel = got.at[pl.ds(start_of[g] - start_of[GATHERED], rows), :]

        @pl.loop(0, halves // 2)
        def _(i):
            two = [lax.rem(z + 1 + 2 * i + q, 4) for q in range(2)]
            for zz in two:
                prod[g % 2, zz, pl.ds(0, rows), :] = jnp.dot(
                    panel[...], halved[zz], preferred_element_type=F32
                )
            for zz in two:
                core_copy(g, i, zz).start()

    def place(part):
        tile = lax.rem(y + part.offset, 4)
        return tile // 2, lax.rem(tile, 2)

    def z_copy(part, k):
        zz = lax.rem(z + k, 4)
        return remote(
            chip.at[zz, pl.ds(part.row, part.rows), :],
            z_got.at[k - 1, pl.ds(part.row_z, part.rows), :],
            z_send,
            z_recv.at[part.number],
            device(y, x, zz, c),
        )

    def x_copy(part, zz):
        to_x = 2 * place(part)[0] + c
        slot = lax.rem(x - to_x + 7, 4)
        return to_x != x, remote(
            chip.at[zz, pl.ds(part.row, part.rows), :],
            x_got.at[slot, zz, pl.ds(part.row_x, part.rows), :],
            x_send.at[part.number],
            x_recv.at[part.group],
            device(y, to_x, z, c),
        )

    def sums_over_x(part):
        return 2 * place(part)[0] + c == x

    def chip_sum(g):
        lanes = pl.ds(pl.multiple_of(c * width, 128), width)
        for i in range(halves):
            zz = lax.rem(z + 1 + i, 4)
            if i % 2 == 0:
                both = core_got.at[pl.ds(0, 2), pl.ds(start_of[g], rows_of[g]), :]
                landed(both, core_recv.at[g, i // 2])
                landed(both, core_send.at[g % 2, i // 2])

            @pl.loop(0, rows_of[g] // step)
            def _(n):
                r = pl.multiple_of(n * step, step)
                at = pl.ds(pl.multiple_of(start_of[g] + r, step), step)
                total = prod[g % 2, zz, pl.ds(r, step), lanes] + core_got[zz, at, :]
                chip[zz, at, :] = total.astype(BF16)

            for part in PARTS:
                if part.group != g:
                    continue
                if part.first == "z":
                    if i < halves - 1:
                        z_copy(part, i + 1).start()
                else:
                    away, copy = x_copy(part, zz)

                    @pl.when(away)
                    def _():
                        copy.start()

    def last_copies(part):
        to_c = place(part)[1]
        if part.first == "z":
            to_x = 2 * place(part)[0] + c
            ends = [(z_total.at[pl.ds(part.row_z, part.rows), :], x, to_x, z)]
        else:
            ends = [
                (x_total.at[zz, pl.ds(part.row_x, part.rows), :], z, x, zz) for zz in range(halves)
            ]
        copies = []
        for src, slot, to_x, to_z in ends:
            dst = last_got.at[slot, pl.ds(part.tile_row, part.rows), :]
            recv = last_recv.at[part.number]
            mine = jnp.logical_and(jnp.logical_and(to_x == x, to_z == z), to_c == c)
            away = remote(
                src, dst, last_send.at[part.number], recv, device(y, to_x, to_z, to_c)
            )
            copies.append((mine, away, pltpu.make_async_copy(src, dst, recv)))
        return copies

    def send_last(part):
        for mine, away, here in last_copies(part):

            @pl.when(mine)
            def _():
                here.start()

            @pl.when(jnp.logical_not(mine))
            def _():
                away.start()

    def wait_last(part):
        if part.first == "z":
            ((mine, away, _),) = last_copies(part)

            @pl.when(jnp.logical_not(mine))
            def _():
                away.wait_send()

        else:
            at = pl.ds(part.row_x, part.rows)
            stays = place(part)[1] == c

            @pl.when(stays)
            def _():
                landed(x_total.at[pl.ds(0, halves - 1), at, :], last_send.at[part.number])

            @pl.when(jnp.logical_not(stays))
            def _():
                landed(x_total.at[:, at, :], last_send.at[part.number])

    def second(g):
        for part in PARTS:
            if part.group != g:
                continue
            if part.first == "z":
                landed(z_got.at[:, pl.ds(part.row_z, part.rows), :], z_recv.at[part.number])

                step = min(part.rows, 64)

                @pl.loop(0, part.rows // step)
                def _(n):
                    total = chip[z, pl.ds(part.row + n * step, step), :].astype(F32)
                    at = pl.ds(part.row_z + n * step, step)
                    for k in range(3):
                        total = total + z_got[k, at, :].astype(F32)
                    z_total[at, :] = total.astype(BF16)

                send_last(part)
            else:

                @pl.when(sums_over_x(part))
                def _():
                    at = pl.ds(part.row_x, part.rows)
                    step = min(part.rows, 64)
                    landed(x_got.at[:, :, at, :], x_recv.at[g])

                    @pl.loop(0, halves * (part.rows // step))
                    def _(n):
                        zz, r = n // (part.rows // step), lax.rem(n, part.rows // step) * step
                        r = pl.multiple_of(r, step)
                        total = chip[zz, pl.ds(part.row + r, step), :].astype(F32)
                        at = pl.ds(part.row_x + r, step)
                        for k in range(3):
                            total = total + x_got[k, zz, at, :].astype(F32)
                        x_total[zz, at, :] = total.astype(BF16)

                    send_last(part)

    own_tile = 2 * (x // 2) + c
    own_offset = lax.rem(own_tile - y + 4, 4)

    def final(g):
        for part in PARTS:
            if part.group != g:
                continue

            @pl.when(own_offset == part.offset)
            def _():
                arrived = last_got.at[:, pl.ds(part.tile_row, part.rows), :]
                landed(arrived, last_recv.at[part.number])

                step = min(part.rows, 64)

                @pl.loop(0, part.rows // step)
                def _(n):
                    at = pl.ds(part.tile_row + n * step, step)
                    total = last_got[0, at, :].astype(F32)
                    for k in range(1, 4):
                        total = total + last_got[k, at, :].astype(F32)
                    out_ref[at, :] = total

    def gathered(g):
        k = g - GATHERED
        span = pl.ds(start_of[g] - start_of[GATHERED], rows_of[g])
        landed(got.at[span, :], ag_recv.at[k])
        for step_on in {0: (2,), 1: range(3, NG - GATHERED)}.get(k, ()):
            for way in range(2):
                gather_copy(way, step_on).start()

    steps = dict(get=gathered, mul=multiply, chip=chip_sum, second=second, final=final)
    for name, g in ORDER:
        steps[name](g)

    for way in range(2):
        landed(got.at[pl.ds(0, (ROWS - width) // 2), :], ag_send.at[way])
    landed(z_got, z_send)
    for part in PARTS:
        if part.first == "z":
            wait_last(part)
        else:
            away, _ = x_copy(part, 0)

            @pl.when(away)
            def _():
                landed(chip.at[:, pl.ds(part.row, part.rows), :], x_send.at[part.number])

            @pl.when(sums_over_x(part))
            def _():
                wait_last(part)


def shards(left_vectors, right_vectors, amplitudes):
    pairs, d_block, c_block = amplitudes.shape
    _, vectors, width = left_vectors.shape
    depth = d_block * vectors
    big = 2 * CH
    dma = pltpu.SemaphoreType.DMA
    turned = pl.pallas_call(
        functools.partial(kernel, (pairs, d_block, c_block, vectors, width)),
        out_shape=jax.ShapeDtypeStruct((width, width), F32),
        in_specs=[
            pl.BlockSpec(memory_space=pltpu.VMEM),
            pl.BlockSpec(memory_space=pl.ANY),
            pl.BlockSpec(memory_space=pl.ANY),
        ],
        out_specs=pl.BlockSpec(memory_space=pltpu.VMEM),
        scratch_shapes=[
            pltpu.VMEM((2, c_block, PB, width), BF16),
            pltpu.VMEM((width // 128, c_block * PB, 128), F32),
            pltpu.VMEM((width // CH, d_block, vectors, CH), BF16),
            pltpu.VMEM((depth, CH), F32),
            pltpu.VMEM((width, depth), BF16),
            pltpu.VMEM((ROWS - width, depth), BF16),
            pltpu.VMEM((pairs // 2, depth, 2 * width), BF16),
            pltpu.VMEM((2, pairs // 2, big, 2 * width), F32),
            pltpu.VMEM((pairs // 2, ROWS, width), F32),
            pltpu.VMEM((pairs // 2, ROWS, width), BF16),
            pltpu.VMEM((3, ROWS_Z, width), BF16),
            pltpu.VMEM((ROWS_Z, width), BF16),
            pltpu.VMEM((3, pairs // 2, ROWS_X, width), BF16),
            pltpu.VMEM((pairs // 2, ROWS_X, width), BF16),
            pltpu.VMEM((4, width, width), BF16),
            dma((2,)),
            dma((width // CH,)),
            dma((2,)),
            dma((NG - GATHERED,)),
            dma((2, 2)),
            dma((NG, 2)),
            dma,
            dma((len(PARTS),)),
            dma((len(PARTS),)),
            dma((NG,)),
            dma((len(PARTS),)),
            dma((len(PARTS),)),
        ],
        compiler_params=pltpu.CompilerParams(
            collective_id=0, has_side_effects=True, vmem_limit_bytes=67_043_328
        ),
    )(amplitudes.reshape(pairs * d_block, c_block), left_vectors, right_vectors)
    return turned.T[None]


def solution(mesh):
    finer = Mesh(
        mesh.devices.reshape(mesh.shape["row"], 2, 2, 4, 2),
        ("row", "col_0", "col_1", "chol_0", "chol_1"),
    )
    placed = (P(None, COL_CHOL, "row"), P(None, COL_CHOL, "row"), P())
    return jax.shard_map(
        shards, mesh=finer, in_specs=placed, out_specs=P(CHOL, "row", COL), check_vma=False
    )
```

```python
import functools

import jax
import jax.numpy as jnp
from jax import lax
from jax.experimental import pallas as pl
from jax.experimental.pallas import tpu as pltpu
from jax.sharding import Mesh
from jax.sharding import PartitionSpec as P

COL = ("col_0", "col_1")
COL_CHOL = ("col_0", "col_1", "chol_0", "chol_1")
CHOL = ("chol_0", "chol_1")
MESH = pl.DeviceIdType.MESH
F32 = jnp.float32
BF16 = jnp.bfloat16
CH = 128
PB = 16

GROUPS = (
    ((0, 0, 256, "z"),),
    ((0, 256, 128, "z"),),
    ((3, 0, 128, "x"), (1, 256, 128, "x")),
    ((3, 128, 128, "z"), (1, 128, 128, "z")),
    ((2, 0, 128, "z"), (2, 256, 128, "z")),
    ((2, 128, 128, "z"),),
    ((3, 256, 64, "z"), (1, 0, 64, "z")),
    ((3, 320, 32, "z"), (3, 352, 32, "x"), (1, 64, 32, "z"), (1, 96, 32, "x")),
)
NG = len(GROUPS)
GATHERED = 2
ORDER = (
    ("mul", 0), ("mul", 1), ("chip", 0), ("chip", 1),
    ("get", 2), ("mul", 2), ("chip", 2),
    ("get", 3), ("mul", 3), ("second", 0), ("chip", 3), ("second", 1), ("second", 2),
    ("get", 4), ("mul", 4), ("chip", 4), ("second", 3), ("final", 0), ("final", 1),
    ("get", 5), ("mul", 5), ("chip", 5), ("final", 2),
    ("get", 6), ("mul", 6), ("chip", 6), ("second", 4),
    ("get", 7), ("mul", 7), ("chip", 7), ("second", 5), ("second", 6), ("second", 7),
    ("final", 3), ("final", 4), ("final", 5), ("final", 6), ("final", 7),
)


class Part:
    def __init__(self, number, group, offset, tile_row, rows, first, row, row_z, row_x):
        self.number, self.group, self.offset, self.tile_row = number, group, offset, tile_row
        self.rows, self.first, self.row, self.row_z, self.row_x = rows, first, row, row_z, row_x


def laid_out():
    parts, row, row_z, row_x = [], 0, 0, 0
    for g, group in enumerate(GROUPS):
        shared = 0
        for offset, tile_row, rows, first in group:
            parts.append(Part(len(parts), g, offset, tile_row, rows, first, row, row_z, row_x))
            row += rows
            if first == "z":
                row_z += rows
            else:
                shared = rows
        row_x += shared
    return parts, row, row_z, row_x


PARTS, ROWS, ROWS_Z, ROWS_X = laid_out()


def where():
    return dict(
        y=lax.axis_index("row"),
        x=lax.axis_index("col_0") * 2 + lax.axis_index("chol_1"),
        z=lax.axis_index("chol_0"),
        c=lax.axis_index("col_1"),
    )


def device(y, x, z, c):
    return (y, x // 2, c, z, lax.rem(x, 2))


def kernel(
    sizes, amp_ref, left_hbm, right_hbm, out_ref,
    left_buf, left_f32, right_buf, right_f32, own, got, halved, prod, core_got, chip, z_got,
    z_total, x_got, x_total, last_got,
    load_sem, right_sem, ag_send, ag_recv, core_send, core_recv, z_send, z_recv, x_send, x_recv,
    last_send, last_recv,
):
    pairs, d_block, c_block, vectors, width = sizes
    depth = d_block * vectors
    me = where()
    y, x, z, c = me["y"], me["x"], me["z"], me["c"]
    up = device(lax.rem(y + 1, 4), x, z, c)
    down = device(lax.rem(y + 3, 4), x, z, c)
    partner = device(y, x, z, 1 - c)

    barrier = pltpu.get_barrier_semaphore()
    others = [up, down, partner]
    others += [device(y, x, lax.rem(z + k, 4), q) for k in (1, 2, 3) for q in (c, 1 - c)]
    others += [device(y, lax.rem(x + k, 4), z, q) for k in (1, 2, 3) for q in (c, 1 - c)]
    for other in others:
        pl.semaphore_signal(barrier, inc=1, device_id=other, device_id_type=MESH)

    def load_right(chunk):
        lanes = pl.ds(chunk * CH, CH)
        return pltpu.make_async_copy(
            right_hbm.at[:, :, lanes], right_buf.at[chunk], right_sem.at[chunk]
        )

    for chunk in (0, 2, 1):
        load_right(chunk).start()

    def load_left(block, slot):
        return pltpu.make_async_copy(
            left_hbm.at[:, pl.ds(pl.multiple_of(block * PB, PB), PB), :],
            left_buf.at[slot],
            load_sem.at[slot],
        )

    load_left(0, 0).start()

    def turn(chunk):
        load_right(chunk).wait()

        @pl.loop(0, d_block, unroll=4)
        def _(d):
            right_f32[pl.ds(d * vectors, vectors), :] = right_buf[chunk, d].astype(F32)

        @pl.loop(0, depth // CH, unroll=6)
        def _(k):
            vecs = CH // d_block
            rows = [
                right_f32[pl.ds(k * vecs + p, d_block, stride=vectors), :] for p in range(vecs)
            ]
            block = jnp.concatenate(rows, axis=0).astype(BF16)
            own[pl.ds(chunk * CH, CH), pl.ds(pl.multiple_of(k * CH, CH), CH)] = block.T

    def remote(src, dst, send, recv, target):
        return pltpu.make_async_remote_copy(
            src_ref=src, dst_ref=dst, send_sem=send, recv_sem=recv, device_id=target,
            device_id_type=MESH,
        )

    rows_of = [sum(p.rows for p in PARTS if p.group == g) for g in range(NG)]
    start_of = [sum(rows_of[:g]) for g in range(NG)]

    def landed(ref, sem):
        pltpu.make_async_copy(ref, ref, sem).wait()

    def gather_copy(way, k):
        target = up if way == 0 else down
        first = start_of[GATHERED]
        half = rows_of[GATHERED + k] // 2
        dst = got.at[pl.ds(start_of[GATHERED + k] - first + way * half, half), :]
        if k in (2, 3):
            at = start_of[GATHERED + k - 2] - first + way * CH + (way * half if k == 3 else 0)
            src = got.at[pl.ds(at, half), :]
        else:
            chunk = min(k, 2) if way == 0 else 2 - min(k, 2)
            past = sum(rows_of[GATHERED + 4 : GATHERED + k]) // 2
            src = own.at[pl.ds(chunk * CH + past, half), :]
        return remote(src, dst, ag_send.at[way], ag_recv.at[k], target)

    turn(0)
    pl.semaphore_wait(barrier, len(others))
    gather_copy(0, 0).start()
    turn(2)
    gather_copy(1, 0).start()
    turn(1)
    gather_copy(0, 1).start()
    gather_copy(1, 1).start()

    @pl.loop(0, vectors // PB)
    def _(block):
        slot = lax.rem(block, 2)
        load_left(block, slot).wait()

        @pl.when(block + 1 < vectors // PB)
        def _():
            load_left(block + 1, 1 - slot).start()

        @pl.loop(0, c_block // 8, unroll=4)
        def _(k):
            part = left_buf[slot, pl.ds(k * 8, 8)].astype(F32)
            for lane in range(width // 128):
                left_f32[lane, pl.ds(pl.multiple_of(k * 8 * PB, 8 * PB), 8 * PB), :] = part[
                    :, :, lane * 128 : (lane + 1) * 128
                ].reshape(8 * PB, 128)

        @pl.loop(0, PB // 2, unroll=8)
        def _(k):
            cols = [
                left_f32[lane, pl.ds(2 * k + q, c_block, stride=PB), :]
                for q in range(2)
                for lane in range(width // 128)
            ]
            vecs = jnp.concatenate(cols, axis=1).astype(BF16)
            half = jnp.dot(amp_ref[...], vecs, preferred_element_type=F32).astype(BF16)
            for q in range(2):
                at = pl.multiple_of((block * PB + 2 * k + q) * d_block, d_block)
                for ij in range(pairs):
                    halved[ij // 2, pl.ds(at, d_block), (ij % 2) * width : (ij % 2 + 1) * width] = (
                        half[ij * d_block : (ij + 1) * d_block, q * width : (q + 1) * width]
                    )

    halves = pairs // 2
    step = 64

    def core_copy(g, pair, zz):
        lanes = pl.ds(pl.multiple_of((1 - c) * width, 128), width)
        return remote(
            prod.at[g % 2, zz, pl.ds(0, rows_of[g]), lanes],
            core_got.at[zz, pl.ds(start_of[g], rows_of[g]), :],
            core_send.at[g % 2, pair],
            core_recv.at[g, pair],
            partner,
        )

    def multiply(g):
        rows = rows_of[g]
        if g < GATHERED:
            panel = own.at[pl.ds(start_of[g], rows), :]
        else:
            panel = got.at[pl.ds(start_of[g] - start_of[GATHERED], rows), :]

        @pl.loop(0, halves // 2)
        def _(i):
            two = [lax.rem(z + 2 + i, 4), lax.rem(z + 1 + 3 * i, 4)]
            for zz in two:
                prod[g % 2, zz, pl.ds(0, rows), :] = jnp.dot(
                    panel[...], halved[zz], preferred_element_type=F32
                )
            for zz in two:
                core_copy(g, i, zz).start()

    def place(part):
        tile = lax.rem(y + part.offset, 4)
        return tile // 2, lax.rem(tile, 2)

    def z_copy(part, k):
        zz = lax.rem(z + k, 4)
        return remote(
            chip.at[zz, pl.ds(part.row, part.rows), :],
            z_got.at[k - 1, pl.ds(part.row_z, part.rows), :],
            z_send,
            z_recv.at[part.number],
            device(y, x, zz, c),
        )

    def x_copy(part, zz):
        to_x = 2 * place(part)[0] + c
        slot = lax.rem(x - to_x + 7, 4)
        return to_x != x, remote(
            chip.at[zz, pl.ds(part.row, part.rows), :],
            x_got.at[slot, zz, pl.ds(part.row_x, part.rows), :],
            x_send.at[part.number],
            x_recv.at[part.group],
            device(y, to_x, z, c),
        )

    def sums_over_x(part):
        return 2 * place(part)[0] + c == x

    def chip_sum(g):
        lanes = pl.ds(pl.multiple_of(c * width, 128), width)
        for i, ahead in enumerate((2, 1, 3, 0)):
            zz = lax.rem(z + ahead, 4)
            if i % 2 == 0:
                both = core_got.at[pl.ds(0, 2), pl.ds(start_of[g], rows_of[g]), :]
                landed(both, core_recv.at[g, i // 2])
                landed(both, core_send.at[g % 2, i // 2])

            @pl.loop(0, rows_of[g] // step)
            def _(n):
                r = pl.multiple_of(n * step, step)
                at = pl.ds(pl.multiple_of(start_of[g] + r, step), step)
                total = prod[g % 2, zz, pl.ds(r, step), lanes] + core_got[zz, at, :]
                chip[zz, at, :] = total.astype(BF16)

            for part in PARTS:
                if part.group != g:
                    continue
                if part.first == "z":
                    if ahead:
                        z_copy(part, ahead).start()
                else:
                    away, copy = x_copy(part, zz)

                    @pl.when(away)
                    def _():
                        copy.start()

    def last_copies(part):
        to_c = place(part)[1]
        if part.first == "z":
            to_x = 2 * place(part)[0] + c
            ends = [(z_total.at[pl.ds(part.row_z, part.rows), :], x, to_x, z)]
        else:
            ends = [
                (x_total.at[zz, pl.ds(part.row_x, part.rows), :], z, x, zz) for zz in range(halves)
            ]
        copies = []
        for src, slot, to_x, to_z in ends:
            dst = last_got.at[slot, pl.ds(part.tile_row, part.rows), :]
            recv = last_recv.at[part.number]
            mine = jnp.logical_and(jnp.logical_and(to_x == x, to_z == z), to_c == c)
            away = remote(
                src, dst, last_send.at[part.number], recv, device(y, to_x, to_z, to_c)
            )
            copies.append((mine, away, pltpu.make_async_copy(src, dst, recv)))
        return copies

    def send_last(part):
        for mine, away, here in last_copies(part):

            @pl.when(mine)
            def _():
                here.start()

            @pl.when(jnp.logical_not(mine))
            def _():
                away.start()

    def wait_last(part):
        if part.first == "z":
            ((mine, away, _),) = last_copies(part)

            @pl.when(jnp.logical_not(mine))
            def _():
                away.wait_send()

        else:
            at = pl.ds(part.row_x, part.rows)
            stays = place(part)[1] == c

            @pl.when(stays)
            def _():
                landed(x_total.at[pl.ds(0, halves - 1), at, :], last_send.at[part.number])

            @pl.when(jnp.logical_not(stays))
            def _():
                landed(x_total.at[:, at, :], last_send.at[part.number])

    def second(g):
        for part in PARTS:
            if part.group != g:
                continue
            if part.first == "z":
                landed(z_got.at[:, pl.ds(part.row_z, part.rows), :], z_recv.at[part.number])

                step = min(part.rows, 64)

                @pl.loop(0, part.rows // step)
                def _(n):
                    total = chip[z, pl.ds(part.row + n * step, step), :].astype(F32)
                    at = pl.ds(part.row_z + n * step, step)
                    for k in range(3):
                        total = total + z_got[k, at, :].astype(F32)
                    z_total[at, :] = total.astype(BF16)

                send_last(part)
            else:

                @pl.when(sums_over_x(part))
                def _():
                    at = pl.ds(part.row_x, part.rows)
                    step = min(part.rows, 64)
                    landed(x_got.at[:, :, at, :], x_recv.at[g])

                    @pl.loop(0, halves * (part.rows // step))
                    def _(n):
                        zz, r = n // (part.rows // step), lax.rem(n, part.rows // step) * step
                        r = pl.multiple_of(r, step)
                        total = chip[zz, pl.ds(part.row + r, step), :].astype(F32)
                        at = pl.ds(part.row_x + r, step)
                        for k in range(3):
                            total = total + x_got[k, zz, at, :].astype(F32)
                        x_total[zz, at, :] = total.astype(BF16)

                    send_last(part)

    own_tile = 2 * (x // 2) + c
    own_offset = lax.rem(own_tile - y + 4, 4)

    def final(g):
        for part in PARTS:
            if part.group != g:
                continue

            @pl.when(own_offset == part.offset)
            def _():
                arrived = last_got.at[:, pl.ds(part.tile_row, part.rows), :]
                landed(arrived, last_recv.at[part.number])

                step = min(part.rows, 64)

                @pl.loop(0, part.rows // step)
                def _(n):
                    at = pl.ds(part.tile_row + n * step, step)
                    total = last_got[0, at, :].astype(F32)
                    for k in range(1, 4):
                        total = total + last_got[k, at, :].astype(F32)
                    out_ref[at, :] = total

    def gathered(g):
        k = g - GATHERED
        span = pl.ds(start_of[g] - start_of[GATHERED], rows_of[g])
        landed(got.at[span, :], ag_recv.at[k])
        for step_on in {0: (2,), 1: range(3, NG - GATHERED)}.get(k, ()):
            for way in range(2):
                gather_copy(way, step_on).start()

    steps = dict(get=gathered, mul=multiply, chip=chip_sum, second=second, final=final)
    for name, g in ORDER:
        steps[name](g)

    for way in range(2):
        landed(got.at[pl.ds(0, (ROWS - width) // 2), :], ag_send.at[way])
    landed(z_got, z_send)
    for part in PARTS:
        if part.first == "z":
            wait_last(part)
        else:
            away, _ = x_copy(part, 0)

            @pl.when(away)
            def _():
                landed(chip.at[:, pl.ds(part.row, part.rows), :], x_send.at[part.number])

            @pl.when(sums_over_x(part))
            def _():
                wait_last(part)


def shards(left_vectors, right_vectors, amplitudes):
    pairs, d_block, c_block = amplitudes.shape
    _, vectors, width = left_vectors.shape
    depth = d_block * vectors
    big = 2 * CH
    dma = pltpu.SemaphoreType.DMA
    turned = pl.pallas_call(
        functools.partial(kernel, (pairs, d_block, c_block, vectors, width)),
        out_shape=jax.ShapeDtypeStruct((width, width), F32),
        in_specs=[
            pl.BlockSpec(memory_space=pltpu.VMEM),
            pl.BlockSpec(memory_space=pl.ANY),
            pl.BlockSpec(memory_space=pl.ANY),
        ],
        out_specs=pl.BlockSpec(memory_space=pltpu.VMEM),
        scratch_shapes=[
            pltpu.VMEM((2, c_block, PB, width), BF16),
            pltpu.VMEM((width // 128, c_block * PB, 128), F32),
            pltpu.VMEM((width // CH, d_block, vectors, CH), BF16),
            pltpu.VMEM((depth, CH), F32),
            pltpu.VMEM((width, depth), BF16),
            pltpu.VMEM((ROWS - width, depth), BF16),
            pltpu.VMEM((pairs // 2, depth, 2 * width), BF16),
            pltpu.VMEM((2, pairs // 2, big, 2 * width), F32),
            pltpu.VMEM((pairs // 2, ROWS, width), F32),
            pltpu.VMEM((pairs // 2, ROWS, width), BF16),
            pltpu.VMEM((3, ROWS_Z, width), BF16),
            pltpu.VMEM((ROWS_Z, width), BF16),
            pltpu.VMEM((3, pairs // 2, ROWS_X, width), BF16),
            pltpu.VMEM((pairs // 2, ROWS_X, width), BF16),
            pltpu.VMEM((4, width, width), BF16),
            dma((2,)),
            dma((width // CH,)),
            dma((2,)),
            dma((NG - GATHERED,)),
            dma((2, 2)),
            dma((NG, 2)),
            dma,
            dma((len(PARTS),)),
            dma((len(PARTS),)),
            dma((NG,)),
            dma((len(PARTS),)),
            dma((len(PARTS),)),
        ],
        compiler_params=pltpu.CompilerParams(
            collective_id=0, has_side_effects=True, vmem_limit_bytes=67_043_328
        ),
    )(amplitudes.reshape(pairs * d_block, c_block), left_vectors, right_vectors)
    return turned.T[None]


def solution(mesh):
    finer = Mesh(
        mesh.devices.reshape(mesh.shape["row"], 2, 2, 4, 2),
        ("row", "col_0", "col_1", "chol_0", "chol_1"),
    )
    placed = (P(None, COL_CHOL, "row"), P(None, COL_CHOL, "row"), P())
    return jax.shard_map(
        shards, mesh=finer, in_specs=placed, out_specs=P(CHOL, "row", COL), check_vma=False
    )
```

```python
import functools

import jax
import jax.numpy as jnp
from jax import lax
from jax.experimental import pallas as pl
from jax.experimental.pallas import tpu as pltpu
from jax.sharding import Mesh
from jax.sharding import PartitionSpec as P

COL = ("col_0", "col_1")
COL_CHOL = ("col_0", "col_1", "chol_0", "chol_1")
CHOL = ("chol_0", "chol_1")
MESH = pl.DeviceIdType.MESH
F32 = jnp.float32
BF16 = jnp.bfloat16
CH = 128
PB = 16

GROUPS = (
    ((0, 0, 256, "z"),),
    ((0, 256, 128, "z"),),
    ((3, 0, 128, "x"), (1, 256, 128, "x")),
    ((3, 128, 128, "z"), (1, 128, 128, "z")),
    ((2, 0, 128, "z"), (2, 256, 128, "z")),
    ((2, 128, 64, "z"), (2, 192, 64, "x")),
    ((3, 256, 64, "z"), (1, 0, 64, "z")),
    ((3, 320, 32, "z"), (3, 352, 32, "x"), (1, 64, 32, "z"), (1, 96, 32, "x")),
)
NG = len(GROUPS)
GATHERED = 2
ORDER = (
    ("mul", 0), ("mul", 1), ("chip", 0), ("chip", 1),
    ("get", 2), ("mul", 2), ("chip", 2),
    ("get", 3), ("mul", 3), ("second", 0), ("chip", 3), ("second", 1), ("second", 2),
    ("get", 4), ("mul", 4), ("chip", 4), ("second", 3), ("final", 0), ("final", 1),
    ("get", 5), ("mul", 5), ("chip", 5), ("final", 2),
    ("get", 6), ("mul", 6), ("chip", 6), ("second", 4),
    ("get", 7), ("mul", 7), ("chip", 7), ("second", 5), ("second", 6), ("second", 7),
    ("final", 3), ("final", 4), ("final", 5), ("final", 6), ("final", 7),
)


class Part:
    def __init__(self, number, group, offset, tile_row, rows, first, row, row_z, row_x):
        self.number, self.group, self.offset, self.tile_row = number, group, offset, tile_row
        self.rows, self.first, self.row, self.row_z, self.row_x = rows, first, row, row_z, row_x


def laid_out():
    parts, row, row_z, row_x = [], 0, 0, 0
    for g, group in enumerate(GROUPS):
        shared = 0
        for offset, tile_row, rows, first in group:
            parts.append(Part(len(parts), g, offset, tile_row, rows, first, row, row_z, row_x))
            row += rows
            if first == "z":
                row_z += rows
            else:
                shared = rows
        row_x += shared
    return parts, row, row_z, row_x


PARTS, ROWS, ROWS_Z, ROWS_X = laid_out()


def where():
    return dict(
        y=lax.axis_index("row"),
        x=lax.axis_index("col_0") * 2 + lax.axis_index("chol_1"),
        z=lax.axis_index("chol_0"),
        c=lax.axis_index("col_1"),
    )


def device(y, x, z, c):
    return (y, x // 2, c, z, lax.rem(x, 2))


def kernel(
    sizes, amp_ref, left_hbm, right_hbm, out_ref,
    left_buf, left_f32, right_buf, right_f32, own, got, halved, prod, core_got, chip, z_got,
    z_total, x_got, x_total, last_got, out_buf,
    load_sem, right_sem, ag_send, ag_recv, core_send, core_recv, z_send, z_recv, x_send, x_recv,
    last_send, last_recv, out_sem,
):
    pairs, d_block, c_block, vectors, width = sizes
    depth = d_block * vectors
    me = where()
    y, x, z, c = me["y"], me["x"], me["z"], me["c"]
    up = device(lax.rem(y + 1, 4), x, z, c)
    down = device(lax.rem(y + 3, 4), x, z, c)
    partner = device(y, x, z, 1 - c)

    barrier = pltpu.get_barrier_semaphore()
    others = [up, down, partner]
    others += [device(y, x, lax.rem(z + k, 4), q) for k in (1, 2, 3) for q in (c, 1 - c)]
    others += [device(y, lax.rem(x + k, 4), z, q) for k in (1, 2, 3) for q in (c, 1 - c)]
    for other in others:
        pl.semaphore_signal(barrier, inc=1, device_id=other, device_id_type=MESH)

    def load_right(chunk):
        lanes = pl.ds(chunk * CH, CH)
        return pltpu.make_async_copy(
            right_hbm.at[:, :, lanes], right_buf.at[chunk], right_sem.at[chunk]
        )

    for chunk in (0, 2, 1):
        load_right(chunk).start()

    def load_left(block, slot):
        return pltpu.make_async_copy(
            left_hbm.at[:, pl.ds(pl.multiple_of(block * PB, PB), PB), :],
            left_buf.at[slot],
            load_sem.at[slot],
        )

    load_left(0, 0).start()

    def turn(chunk):
        load_right(chunk).wait()

        @pl.loop(0, d_block, unroll=4)
        def _(d):
            right_f32[pl.ds(d * vectors, vectors), :] = right_buf[chunk, d].astype(F32)

        @pl.loop(0, depth // CH, unroll=6)
        def _(k):
            vecs = CH // d_block
            rows = [
                right_f32[pl.ds(k * vecs + p, d_block, stride=vectors), :] for p in range(vecs)
            ]
            block = jnp.concatenate(rows, axis=0).astype(BF16)
            own[pl.ds(chunk * CH, CH), pl.ds(pl.multiple_of(k * CH, CH), CH)] = block.T

    def remote(src, dst, send, recv, target):
        return pltpu.make_async_remote_copy(
            src_ref=src, dst_ref=dst, send_sem=send, recv_sem=recv, device_id=target,
            device_id_type=MESH,
        )

    rows_of = [sum(p.rows for p in PARTS if p.group == g) for g in range(NG)]
    start_of = [sum(rows_of[:g]) for g in range(NG)]

    def landed(ref, sem):
        pltpu.make_async_copy(ref, ref, sem).wait()

    def gather_copy(way, k):
        target = up if way == 0 else down
        first = start_of[GATHERED]
        half = rows_of[GATHERED + k] // 2
        dst = got.at[pl.ds(start_of[GATHERED + k] - first + way * half, half), :]
        if k in (2, 3):
            at = start_of[GATHERED + k - 2] - first + way * CH + (way * half if k == 3 else 0)
            src = got.at[pl.ds(at, half), :]
        else:
            chunk = min(k, 2) if way == 0 else 2 - min(k, 2)
            past = sum(rows_of[GATHERED + 4 : GATHERED + k]) // 2
            src = own.at[pl.ds(chunk * CH + past, half), :]
        return remote(src, dst, ag_send.at[way], ag_recv.at[k], target)

    turn(0)
    pl.semaphore_wait(barrier, len(others))
    gather_copy(0, 0).start()
    turn(2)
    gather_copy(1, 0).start()
    turn(1)
    gather_copy(0, 1).start()
    gather_copy(1, 1).start()

    @pl.loop(0, vectors // PB)
    def _(block):
        slot = lax.rem(block, 2)
        load_left(block, slot).wait()

        @pl.when(block + 1 < vectors // PB)
        def _():
            load_left(block + 1, 1 - slot).start()

        @pl.loop(0, c_block // 8, unroll=4)
        def _(k):
            part = left_buf[slot, pl.ds(k * 8, 8)].astype(F32)
            for lane in range(width // 128):
                left_f32[lane, pl.ds(pl.multiple_of(k * 8 * PB, 8 * PB), 8 * PB), :] = part[
                    :, :, lane * 128 : (lane + 1) * 128
                ].reshape(8 * PB, 128)

        @pl.loop(0, PB // 2, unroll=8)
        def _(k):
            cols = [
                left_f32[lane, pl.ds(2 * k + q, c_block, stride=PB), :]
                for q in range(2)
                for lane in range(width // 128)
            ]
            vecs = jnp.concatenate(cols, axis=1).astype(BF16)
            half = jnp.dot(amp_ref[...], vecs, preferred_element_type=F32).astype(BF16)
            for q in range(2):
                at = pl.multiple_of((block * PB + 2 * k + q) * d_block, d_block)
                for ij in range(pairs):
                    halved[ij // 2, pl.ds(at, d_block), (ij % 2) * width : (ij % 2 + 1) * width] = (
                        half[ij * d_block : (ij + 1) * d_block, q * width : (q + 1) * width]
                    )

    halves = pairs // 2
    step = 64

    def core_copy(g, pair, zz):
        lanes = pl.ds(pl.multiple_of((1 - c) * width, 128), width)
        return remote(
            prod.at[g % 2, zz, pl.ds(0, rows_of[g]), lanes],
            core_got.at[zz, pl.ds(start_of[g], rows_of[g]), :],
            core_send.at[g % 2, pair],
            core_recv.at[g, pair],
            partner,
        )

    def multiply(g):
        rows = rows_of[g]
        if g < GATHERED:
            panel = own.at[pl.ds(start_of[g], rows), :]
        else:
            panel = got.at[pl.ds(start_of[g] - start_of[GATHERED], rows), :]

        @pl.loop(0, halves // 2)
        def _(i):
            two = [lax.rem(z + 2 + i, 4), lax.rem(z + 1 + 3 * i, 4)]
            for zz in two:
                prod[g % 2, zz, pl.ds(0, rows), :] = jnp.dot(
                    panel[...], halved[zz], preferred_element_type=F32
                )
            for zz in two:
                core_copy(g, i, zz).start()

    def place(part):
        tile = lax.rem(y + part.offset, 4)
        return tile // 2, lax.rem(tile, 2)

    def z_copy(part, k):
        zz = lax.rem(z + k, 4)
        return remote(
            chip.at[zz, pl.ds(part.row, part.rows), :],
            z_got.at[k - 1, pl.ds(part.row_z, part.rows), :],
            z_send,
            z_recv.at[part.number],
            device(y, x, zz, c),
        )

    def x_copy(part, zz):
        to_x = 2 * place(part)[0] + c
        slot = lax.rem(x - to_x + 7, 4)
        return to_x != x, remote(
            chip.at[zz, pl.ds(part.row, part.rows), :],
            x_got.at[slot, zz, pl.ds(part.row_x, part.rows), :],
            x_send.at[part.number],
            x_recv.at[part.group],
            device(y, to_x, z, c),
        )

    def sums_over_x(part):
        return 2 * place(part)[0] + c == x

    def chip_sum(g):
        lanes = pl.ds(pl.multiple_of(c * width, 128), width)
        for i, ahead in enumerate((2, 1, 3, 0)):
            zz = lax.rem(z + ahead, 4)
            if i % 2 == 0:
                both = core_got.at[pl.ds(0, 2), pl.ds(start_of[g], rows_of[g]), :]
                landed(both, core_recv.at[g, i // 2])
                landed(both, core_send.at[g % 2, i // 2])

            @pl.loop(0, rows_of[g] // step)
            def _(n):
                r = pl.multiple_of(n * step, step)
                at = pl.ds(pl.multiple_of(start_of[g] + r, step), step)
                total = prod[g % 2, zz, pl.ds(r, step), lanes] + core_got[zz, at, :]
                chip[zz, at, :] = total.astype(BF16)

            for part in PARTS:
                if part.group != g:
                    continue
                if part.first == "z":
                    if ahead:
                        z_copy(part, ahead).start()
                else:
                    away, copy = x_copy(part, zz)

                    @pl.when(away)
                    def _():
                        copy.start()

    def last_copies(part):
        to_c = place(part)[1]
        if part.first == "z":
            to_x = 2 * place(part)[0] + c
            ends = [(z_total.at[pl.ds(part.row_z, part.rows), :], x, to_x, z)]
        else:
            ends = [
                (x_total.at[zz, pl.ds(part.row_x, part.rows), :], z, x, zz) for zz in range(halves)
            ]
        copies = []
        for src, slot, to_x, to_z in ends:
            dst = last_got.at[slot, pl.ds(part.tile_row, part.rows), :]
            recv = last_recv.at[part.number]
            mine = jnp.logical_and(jnp.logical_and(to_x == x, to_z == z), to_c == c)
            away = remote(
                src, dst, last_send.at[part.number], recv, device(y, to_x, to_z, to_c)
            )
            copies.append((mine, away, pltpu.make_async_copy(src, dst, recv)))
        return copies

    def send_last(part):
        for mine, away, here in last_copies(part):

            @pl.when(mine)
            def _():
                here.start()

            @pl.when(jnp.logical_not(mine))
            def _():
                away.start()

    def wait_last(part):
        if part.first == "z":
            ((mine, away, _),) = last_copies(part)

            @pl.when(jnp.logical_not(mine))
            def _():
                away.wait_send()

        else:
            at = pl.ds(part.row_x, part.rows)
            stays = place(part)[1] == c

            @pl.when(stays)
            def _():
                landed(x_total.at[pl.ds(0, halves - 1), at, :], last_send.at[part.number])

            @pl.when(jnp.logical_not(stays))
            def _():
                landed(x_total.at[:, at, :], last_send.at[part.number])

    def second(g):
        for part in PARTS:
            if part.group != g:
                continue
            if part.first == "z":
                landed(z_got.at[:, pl.ds(part.row_z, part.rows), :], z_recv.at[part.number])

                step = min(part.rows, 64)

                @pl.loop(0, part.rows // step)
                def _(n):
                    total = chip[z, pl.ds(part.row + n * step, step), :].astype(F32)
                    at = pl.ds(part.row_z + n * step, step)
                    for k in range(3):
                        total = total + z_got[k, at, :].astype(F32)
                    z_total[at, :] = total.astype(BF16)

                send_last(part)
            else:

                @pl.when(sums_over_x(part))
                def _():
                    at = pl.ds(part.row_x, part.rows)
                    step = min(part.rows, 64)
                    landed(x_got.at[:, :, at, :], x_recv.at[g])

                    @pl.loop(0, halves * (part.rows // step))
                    def _(n):
                        zz, r = n // (part.rows // step), lax.rem(n, part.rows // step) * step
                        r = pl.multiple_of(r, step)
                        total = chip[zz, pl.ds(part.row + r, step), :].astype(F32)
                        at = pl.ds(part.row_x + r, step)
                        for k in range(3):
                            total = total + x_got[k, zz, at, :].astype(F32)
                        x_total[zz, at, :] = total.astype(BF16)

                    send_last(part)

    own_tile = 2 * (x // 2) + c
    own_offset = lax.rem(own_tile - y + 4, 4)

    def out_copy(part):
        span = pl.ds(part.tile_row, part.rows)
        return pltpu.make_async_copy(out_buf.at[span, :], out_ref.at[span, :], out_sem)

    def final(g):
        for part in PARTS:
            if part.group != g:
                continue

            @pl.when(own_offset == part.offset)
            def _():
                arrived = last_got.at[:, pl.ds(part.tile_row, part.rows), :]
                landed(arrived, last_recv.at[part.number])

                step = min(part.rows, 64)

                @pl.loop(0, part.rows // step)
                def _(n):
                    at = pl.ds(part.tile_row + n * step, step)
                    total = last_got[0, at, :].astype(F32)
                    for k in range(1, 4):
                        total = total + last_got[k, at, :].astype(F32)
                    out_buf[at, :] = total

                out_copy(part).start()

    def gathered(g):
        k = g - GATHERED
        span = pl.ds(start_of[g] - start_of[GATHERED], rows_of[g])
        landed(got.at[span, :], ag_recv.at[k])
        for step_on in {0: (2,), 1: range(3, NG - GATHERED)}.get(k, ()):
            for way in range(2):
                gather_copy(way, step_on).start()

    steps = dict(get=gathered, mul=multiply, chip=chip_sum, second=second, final=final)
    for name, g in ORDER:
        steps[name](g)

    for way in range(2):
        landed(got.at[pl.ds(0, (ROWS - width) // 2), :], ag_send.at[way])
    landed(z_got, z_send)
    landed(out_buf, out_sem)
    for part in PARTS:
        if part.first == "z":
            wait_last(part)
        else:
            away, _ = x_copy(part, 0)

            @pl.when(away)
            def _():
                landed(chip.at[:, pl.ds(part.row, part.rows), :], x_send.at[part.number])

            @pl.when(sums_over_x(part))
            def _():
                wait_last(part)


def shards(left_vectors, right_vectors, amplitudes):
    pairs, d_block, c_block = amplitudes.shape
    _, vectors, width = left_vectors.shape
    depth = d_block * vectors
    big = 2 * CH
    dma = pltpu.SemaphoreType.DMA
    turned = pl.pallas_call(
        functools.partial(kernel, (pairs, d_block, c_block, vectors, width)),
        out_shape=jax.ShapeDtypeStruct((width, width), F32),
        in_specs=[
            pl.BlockSpec(memory_space=pltpu.VMEM),
            pl.BlockSpec(memory_space=pl.ANY),
            pl.BlockSpec(memory_space=pl.ANY),
        ],
        out_specs=pl.BlockSpec(memory_space=pl.ANY),
        scratch_shapes=[
            pltpu.VMEM((2, c_block, PB, width), BF16),
            pltpu.VMEM((width // 128, c_block * PB, 128), F32),
            pltpu.VMEM((width // CH, d_block, vectors, CH), BF16),
            pltpu.VMEM((depth, CH), F32),
            pltpu.VMEM((width, depth), BF16),
            pltpu.VMEM((ROWS - width, depth), BF16),
            pltpu.VMEM((pairs // 2, depth, 2 * width), BF16),
            pltpu.VMEM((2, pairs // 2, big, 2 * width), F32),
            pltpu.VMEM((pairs // 2, ROWS, width), F32),
            pltpu.VMEM((pairs // 2, ROWS, width), BF16),
            pltpu.VMEM((3, ROWS_Z, width), BF16),
            pltpu.VMEM((ROWS_Z, width), BF16),
            pltpu.VMEM((3, pairs // 2, ROWS_X, width), BF16),
            pltpu.VMEM((pairs // 2, ROWS_X, width), BF16),
            pltpu.VMEM((4, width, width), BF16),
            pltpu.VMEM((width, width), F32),
            dma((2,)),
            dma((width // CH,)),
            dma((2,)),
            dma((NG - GATHERED,)),
            dma((2, 2)),
            dma((NG, 2)),
            dma,
            dma((len(PARTS),)),
            dma((len(PARTS),)),
            dma((NG,)),
            dma((len(PARTS),)),
            dma((len(PARTS),)),
            dma,
        ],
        compiler_params=pltpu.CompilerParams(
            collective_id=0, has_side_effects=True, vmem_limit_bytes=67_043_328
        ),
    )(amplitudes.reshape(pairs * d_block, c_block), left_vectors, right_vectors)
    return turned.T[None]


def solution(mesh):
    finer = Mesh(
        mesh.devices.reshape(mesh.shape["row"], 2, 2, 4, 2),
        ("row", "col_0", "col_1", "chol_0", "chol_1"),
    )
    placed = (P(None, COL_CHOL, "row"), P(None, COL_CHOL, "row"), P())
    return jax.shard_map(
        shards, mesh=finer, in_specs=placed, out_specs=P(CHOL, "row", COL), check_vma=False
    )
```

```python
import functools

import jax
import jax.numpy as jnp
from jax import lax
from jax.experimental import pallas as pl
from jax.experimental.pallas import tpu as pltpu
from jax.sharding import Mesh
from jax.sharding import PartitionSpec as P

COL = ("col_0", "col_1")
COL_CHOL = ("col_0", "col_1", "chol_0", "chol_1")
CHOL = ("chol_0", "chol_1")
MESH = pl.DeviceIdType.MESH
F32 = jnp.float32
BF16 = jnp.bfloat16
CH = 128
PB = 16

GROUPS = (
    ((0, 0, 256, "z"),),
    ((0, 256, 128, "z"),),
    ((3, 0, 128, "x"), (1, 256, 128, "x")),
    ((3, 128, 128, "z"), (1, 128, 128, "z")),
    ((2, 0, 128, "z"), (2, 256, 128, "x")),
    ((2, 128, 64, "z"), (2, 192, 64, "x")),
    ((3, 256, 64, "z"), (1, 0, 64, "z")),
    ((3, 320, 32, "z"), (3, 352, 32, "x"), (1, 64, 32, "z"), (1, 96, 32, "x")),
)
NG = len(GROUPS)
GATHERED = 2
ORDER = (
    ("mul", 0), ("mul", 1), ("chip", 0), ("chip", 1),
    ("get", 2), ("mul", 2), ("chip", 2),
    ("get", 3), ("mul", 3), ("second", 0), ("chip", 3), ("second", 1), ("second", 2),
    ("get", 4), ("mul", 4), ("chip", 4), ("second", 3), ("final", 0), ("final", 1),
    ("get", 5), ("mul", 5), ("chip", 5), ("final", 2),
    ("get", 6), ("mul", 6), ("chip", 6), ("second", 4),
    ("get", 7), ("mul", 7), ("chip", 7), ("second", 5), ("second", 6), ("second", 7),
    ("final", 3), ("final", 4), ("final", 5), ("final", 6), ("final", 7),
)


class Part:
    def __init__(self, number, group, offset, tile_row, rows, first, row, row_z, row_x):
        self.number, self.group, self.offset, self.tile_row = number, group, offset, tile_row
        self.rows, self.first, self.row, self.row_z, self.row_x = rows, first, row, row_z, row_x


def laid_out():
    parts, row, row_z, row_x = [], 0, 0, 0
    for g, group in enumerate(GROUPS):
        shared = 0
        for offset, tile_row, rows, first in group:
            parts.append(Part(len(parts), g, offset, tile_row, rows, first, row, row_z, row_x))
            row += rows
            if first == "z":
                row_z += rows
            else:
                shared = rows
        row_x += shared
    return parts, row, row_z, row_x


PARTS, ROWS, ROWS_Z, ROWS_X = laid_out()


def where():
    return dict(
        y=lax.axis_index("row"),
        x=lax.axis_index("col_0") * 2 + lax.axis_index("chol_1"),
        z=lax.axis_index("chol_0"),
        c=lax.axis_index("col_1"),
    )


def device(y, x, z, c):
    return (y, x // 2, c, z, lax.rem(x, 2))


def kernel(
    sizes, amp_ref, left_hbm, right_hbm, out_ref,
    left_buf, left_f32, right_buf, right_f32, own, got, halved, prod, core_got, chip, z_got,
    z_total, x_got, x_total, last_got, out_buf,
    load_sem, right_sem, ag_send, ag_recv, core_send, core_recv, z_send, z_recv, x_send, x_recv,
    last_send, last_recv, out_sem,
):
    pairs, d_block, c_block, vectors, width = sizes
    depth = d_block * vectors
    me = where()
    y, x, z, c = me["y"], me["x"], me["z"], me["c"]
    up = device(lax.rem(y + 1, 4), x, z, c)
    down = device(lax.rem(y + 3, 4), x, z, c)
    partner = device(y, x, z, 1 - c)

    barrier = pltpu.get_barrier_semaphore()
    others = [up, down, partner]
    others += [device(y, x, lax.rem(z + k, 4), q) for k in (1, 2, 3) for q in (c, 1 - c)]
    others += [device(y, lax.rem(x + k, 4), z, q) for k in (1, 2, 3) for q in (c, 1 - c)]
    for other in others:
        pl.semaphore_signal(barrier, inc=1, device_id=other, device_id_type=MESH)

    def load_right(chunk):
        lanes = pl.ds(chunk * CH, CH)
        return pltpu.make_async_copy(
            right_hbm.at[:, :, lanes], right_buf.at[chunk], right_sem.at[chunk]
        )

    for chunk in (0, 2, 1):
        load_right(chunk).start()

    def load_left(block, slot):
        return pltpu.make_async_copy(
            left_hbm.at[:, pl.ds(pl.multiple_of(block * PB, PB), PB), :],
            left_buf.at[slot],
            load_sem.at[slot],
        )

    load_left(0, 0).start()

    def turn(chunk):
        load_right(chunk).wait()

        @pl.loop(0, d_block, unroll=4)
        def _(d):
            right_f32[pl.ds(d * vectors, vectors), :] = right_buf[chunk, d].astype(F32)

        @pl.loop(0, depth // CH, unroll=6)
        def _(k):
            vecs = CH // d_block
            rows = [
                right_f32[pl.ds(k * vecs + p, d_block, stride=vectors), :] for p in range(vecs)
            ]
            block = jnp.concatenate(rows, axis=0).astype(BF16)
            own[pl.ds(chunk * CH, CH), pl.ds(pl.multiple_of(k * CH, CH), CH)] = block.T

    def remote(src, dst, send, recv, target):
        return pltpu.make_async_remote_copy(
            src_ref=src, dst_ref=dst, send_sem=send, recv_sem=recv, device_id=target,
            device_id_type=MESH,
        )

    rows_of = [sum(p.rows for p in PARTS if p.group == g) for g in range(NG)]
    start_of = [sum(rows_of[:g]) for g in range(NG)]

    def landed(ref, sem):
        pltpu.make_async_copy(ref, ref, sem).wait()

    def gather_copy(way, k):
        target = up if way == 0 else down
        first = start_of[GATHERED]
        half = rows_of[GATHERED + k] // 2
        dst = got.at[pl.ds(start_of[GATHERED + k] - first + way * half, half), :]
        if k in (2, 3):
            at = start_of[GATHERED + k - 2] - first + way * CH + (way * half if k == 3 else 0)
            src = got.at[pl.ds(at, half), :]
        else:
            chunk = min(k, 2) if way == 0 else 2 - min(k, 2)
            past = sum(rows_of[GATHERED + 4 : GATHERED + k]) // 2
            src = own.at[pl.ds(chunk * CH + past, half), :]
        return remote(src, dst, ag_send.at[way], ag_recv.at[k], target)

    turn(0)
    pl.semaphore_wait(barrier, len(others))
    gather_copy(0, 0).start()
    turn(2)
    gather_copy(1, 0).start()
    turn(1)
    gather_copy(0, 1).start()
    gather_copy(1, 1).start()

    @pl.loop(0, vectors // PB)
    def _(block):
        slot = lax.rem(block, 2)
        load_left(block, slot).wait()

        @pl.when(block + 1 < vectors // PB)
        def _():
            load_left(block + 1, 1 - slot).start()

        @pl.loop(0, c_block // 8, unroll=4)
        def _(k):
            part = left_buf[slot, pl.ds(k * 8, 8)].astype(F32)
            for lane in range(width // 128):
                left_f32[lane, pl.ds(pl.multiple_of(k * 8 * PB, 8 * PB), 8 * PB), :] = part[
                    :, :, lane * 128 : (lane + 1) * 128
                ].reshape(8 * PB, 128)

        @pl.loop(0, PB // 2, unroll=8)
        def _(k):
            cols = [
                left_f32[lane, pl.ds(2 * k + q, c_block, stride=PB), :]
                for q in range(2)
                for lane in range(width // 128)
            ]
            vecs = jnp.concatenate(cols, axis=1).astype(BF16)
            half = jnp.dot(amp_ref[...], vecs, preferred_element_type=F32).astype(BF16)
            for q in range(2):
                at = pl.multiple_of((block * PB + 2 * k + q) * d_block, d_block)
                for ij in range(pairs):
                    halved[ij // 2, pl.ds(at, d_block), (ij % 2) * width : (ij % 2 + 1) * width] = (
                        half[ij * d_block : (ij + 1) * d_block, q * width : (q + 1) * width]
                    )

    halves = pairs // 2
    step = 64

    def core_copy(g, pair, zz):
        lanes = pl.ds(pl.multiple_of((1 - c) * width, 128), width)
        return remote(
            prod.at[g % 2, zz, pl.ds(0, rows_of[g]), lanes],
            core_got.at[zz, pl.ds(start_of[g], rows_of[g]), :],
            core_send.at[g % 2, pair],
            core_recv.at[g, pair],
            partner,
        )

    def multiply(g):
        rows = rows_of[g]
        if g < GATHERED:
            panel = own.at[pl.ds(start_of[g], rows), :]
        else:
            panel = got.at[pl.ds(start_of[g] - start_of[GATHERED], rows), :]

        @pl.loop(0, halves // 2)
        def _(i):
            two = [lax.rem(z + 2 + i, 4), lax.rem(z + 1 + 3 * i, 4)]
            for zz in two:
                prod[g % 2, zz, pl.ds(0, rows), :] = jnp.dot(
                    panel[...], halved[zz], preferred_element_type=F32
                )
            for zz in two:
                core_copy(g, i, zz).start()

    def place(part):
        tile = lax.rem(y + part.offset, 4)
        return tile // 2, lax.rem(tile, 2)

    def z_copy(part, k):
        zz = lax.rem(z + k, 4)
        return remote(
            chip.at[zz, pl.ds(part.row, part.rows), :],
            z_got.at[k - 1, pl.ds(part.row_z, part.rows), :],
            z_send,
            z_recv.at[part.number],
            device(y, x, zz, c),
        )

    def x_copy(part, zz):
        to_x = 2 * place(part)[0] + c
        slot = lax.rem(x - to_x + 7, 4)
        return to_x != x, remote(
            chip.at[zz, pl.ds(part.row, part.rows), :],
            x_got.at[slot, zz, pl.ds(part.row_x, part.rows), :],
            x_send.at[part.number],
            x_recv.at[part.group],
            device(y, to_x, z, c),
        )

    def sums_over_x(part):
        return 2 * place(part)[0] + c == x

    def chip_sum(g):
        lanes = pl.ds(pl.multiple_of(c * width, 128), width)
        for i, ahead in enumerate((2, 1, 3, 0)):
            zz = lax.rem(z + ahead, 4)
            if i % 2 == 0:
                both = core_got.at[pl.ds(0, 2), pl.ds(start_of[g], rows_of[g]), :]
                landed(both, core_recv.at[g, i // 2])
                landed(both, core_send.at[g % 2, i // 2])

            @pl.loop(0, rows_of[g] // step)
            def _(n):
                r = pl.multiple_of(n * step, step)
                at = pl.ds(pl.multiple_of(start_of[g] + r, step), step)
                total = prod[g % 2, zz, pl.ds(r, step), lanes] + core_got[zz, at, :]
                chip[zz, at, :] = total.astype(BF16)

            for part in PARTS:
                if part.group != g:
                    continue
                if part.first == "z":
                    if ahead:
                        z_copy(part, ahead).start()
                else:
                    away, copy = x_copy(part, zz)

                    @pl.when(away)
                    def _():
                        copy.start()

    def last_copies(part):
        to_c = place(part)[1]
        if part.first == "z":
            to_x = 2 * place(part)[0] + c
            ends = [(z_total.at[pl.ds(part.row_z, part.rows), :], x, to_x, z)]
        else:
            ends = [
                (x_total.at[zz, pl.ds(part.row_x, part.rows), :], z, x, zz) for zz in range(halves)
            ]
        copies = []
        for src, slot, to_x, to_z in ends:
            dst = last_got.at[slot, pl.ds(part.tile_row, part.rows), :]
            recv = last_recv.at[part.number]
            mine = jnp.logical_and(jnp.logical_and(to_x == x, to_z == z), to_c == c)
            away = remote(
                src, dst, last_send.at[part.number], recv, device(y, to_x, to_z, to_c)
            )
            copies.append((mine, away, pltpu.make_async_copy(src, dst, recv)))
        return copies

    def send_last(part):
        for mine, away, here in last_copies(part):

            @pl.when(mine)
            def _():
                here.start()

            @pl.when(jnp.logical_not(mine))
            def _():
                away.start()

    def wait_last(part):
        if part.first == "z":
            ((mine, away, _),) = last_copies(part)

            @pl.when(jnp.logical_not(mine))
            def _():
                away.wait_send()

        else:
            at = pl.ds(part.row_x, part.rows)
            stays = place(part)[1] == c

            @pl.when(stays)
            def _():
                landed(x_total.at[pl.ds(0, halves - 1), at, :], last_send.at[part.number])

            @pl.when(jnp.logical_not(stays))
            def _():
                landed(x_total.at[:, at, :], last_send.at[part.number])

    def second(g):
        for part in PARTS:
            if part.group != g:
                continue
            if part.first == "z":
                landed(z_got.at[:, pl.ds(part.row_z, part.rows), :], z_recv.at[part.number])

                step = min(part.rows, 64)

                @pl.loop(0, part.rows // step)
                def _(n):
                    total = chip[z, pl.ds(part.row + n * step, step), :].astype(F32)
                    at = pl.ds(part.row_z + n * step, step)
                    for k in range(3):
                        total = total + z_got[k, at, :].astype(F32)
                    z_total[at, :] = total.astype(BF16)

                send_last(part)
            else:

                @pl.when(sums_over_x(part))
                def _():
                    at = pl.ds(part.row_x, part.rows)
                    step = min(part.rows, 64)
                    landed(x_got.at[:, :, at, :], x_recv.at[g])

                    @pl.loop(0, halves * (part.rows // step))
                    def _(n):
                        zz, r = n // (part.rows // step), lax.rem(n, part.rows // step) * step
                        r = pl.multiple_of(r, step)
                        total = chip[zz, pl.ds(part.row + r, step), :].astype(F32)
                        at = pl.ds(part.row_x + r, step)
                        for k in range(3):
                            total = total + x_got[k, zz, at, :].astype(F32)
                        x_total[zz, at, :] = total.astype(BF16)

                    send_last(part)

    own_tile = 2 * (x // 2) + c
    own_offset = lax.rem(own_tile - y + 4, 4)

    def out_copy(part):
        span = pl.ds(part.tile_row, part.rows)
        return pltpu.make_async_copy(out_buf.at[span, :], out_ref.at[span, :], out_sem)

    def final(g):
        for part in PARTS:
            if part.group != g:
                continue

            @pl.when(own_offset == part.offset)
            def _():
                arrived = last_got.at[:, pl.ds(part.tile_row, part.rows), :]
                landed(arrived, last_recv.at[part.number])

                step = min(part.rows, 64)

                @pl.loop(0, part.rows // step)
                def _(n):
                    at = pl.ds(part.tile_row + n * step, step)
                    total = last_got[0, at, :].astype(F32)
                    for k in range(1, 4):
                        total = total + last_got[k, at, :].astype(F32)
                    out_buf[at, :] = total

                out_copy(part).start()

    def gathered(g):
        k = g - GATHERED
        span = pl.ds(start_of[g] - start_of[GATHERED], rows_of[g])
        landed(got.at[span, :], ag_recv.at[k])
        for step_on in {0: (2,), 1: range(3, NG - GATHERED)}.get(k, ()):
            for way in range(2):
                gather_copy(way, step_on).start()

    steps = dict(get=gathered, mul=multiply, chip=chip_sum, second=second, final=final)
    for name, g in ORDER:
        steps[name](g)

    for way in range(2):
        landed(got.at[pl.ds(0, (ROWS - width) // 2), :], ag_send.at[way])
    landed(z_got, z_send)
    landed(out_buf, out_sem)
    for part in PARTS:
        if part.first == "z":
            wait_last(part)
        else:
            away, _ = x_copy(part, 0)

            @pl.when(away)
            def _():
                landed(chip.at[:, pl.ds(part.row, part.rows), :], x_send.at[part.number])

            @pl.when(sums_over_x(part))
            def _():
                wait_last(part)


def shards(left_vectors, right_vectors, amplitudes):
    pairs, d_block, c_block = amplitudes.shape
    _, vectors, width = left_vectors.shape
    depth = d_block * vectors
    big = 2 * CH
    dma = pltpu.SemaphoreType.DMA
    turned = pl.pallas_call(
        functools.partial(kernel, (pairs, d_block, c_block, vectors, width)),
        out_shape=jax.ShapeDtypeStruct((width, width), F32),
        in_specs=[
            pl.BlockSpec(memory_space=pltpu.VMEM),
            pl.BlockSpec(memory_space=pl.ANY),
            pl.BlockSpec(memory_space=pl.ANY),
        ],
        out_specs=pl.BlockSpec(memory_space=pl.ANY),
        scratch_shapes=[
            pltpu.VMEM((2, c_block, PB, width), BF16),
            pltpu.VMEM((width // 128, c_block * PB, 128), F32),
            pltpu.VMEM((width // CH, d_block, vectors, CH), BF16),
            pltpu.VMEM((depth, CH), F32),
            pltpu.VMEM((width, depth), BF16),
            pltpu.VMEM((ROWS - width, depth), BF16),
            pltpu.VMEM((pairs // 2, depth, 2 * width), BF16),
            pltpu.VMEM((2, pairs // 2, big, 2 * width), F32),
            pltpu.VMEM((pairs // 2, ROWS, width), F32),
            pltpu.VMEM((pairs // 2, ROWS, width), BF16),
            pltpu.VMEM((3, ROWS_Z, width), BF16),
            pltpu.VMEM((ROWS_Z, width), BF16),
            pltpu.VMEM((3, pairs // 2, ROWS_X, width), BF16),
            pltpu.VMEM((pairs // 2, ROWS_X, width), BF16),
            pltpu.VMEM((4, width, width), BF16),
            pltpu.VMEM((width, width), F32),
            dma((2,)),
            dma((width // CH,)),
            dma((2,)),
            dma((NG - GATHERED,)),
            dma((2, 2)),
            dma((NG, 2)),
            dma,
            dma((len(PARTS),)),
            dma((len(PARTS),)),
            dma((NG,)),
            dma((len(PARTS),)),
            dma((len(PARTS),)),
            dma,
        ],
        compiler_params=pltpu.CompilerParams(
            collective_id=0, has_side_effects=True, vmem_limit_bytes=67_043_328
        ),
    )(amplitudes.reshape(pairs * d_block, c_block), left_vectors, right_vectors)
    return turned.T[None]


def solution(mesh):
    finer = Mesh(
        mesh.devices.reshape(mesh.shape["row"], 2, 2, 4, 2),
        ("row", "col_0", "col_1", "chol_0", "chol_1"),
    )
    placed = (P(None, COL_CHOL, "row"), P(None, COL_CHOL, "row"), P())
    return jax.shard_map(
        shards, mesh=finer, in_specs=placed, out_specs=P(CHOL, "row", COL), check_vma=False
    )
```
